128 devices in a mesh: batch: 16 (over z, y_lo, core), row: 4 (over x), col: 2 (over y_hi).
Axes of the slice: x: 4, y: 4 (y_hi: 2, y_lo: 2; y = y_hi * 2 + y_lo), z: 4, core: 2. Of those that a mesh axis runs over, the one named last changes fastest.
Arguments:
- features: bfloat16 [16, 64, 256, 320], P('batch', 'row', 'col'), may hold values from -6 to 6
- first_kernel: bfloat16 [3, 3, 320, 320], replicated, may hold values from -0.109375 to 0.109375
- second_kernel: bfloat16 [3, 3, 320, 320], replicated, may hold values from -0.109375 to 0.109375
- first_gain: float32 [320], replicated, may hold values from 0.5 to 1.5
- first_shift: float32 [320], replicated, may hold values from -3 to 3
- second_gain: float32 [320], replicated, may hold values from 0.5 to 1.5
- second_shift: float32 [320], replicated, may hold values from -3 to 3
- upstream: bfloat16 [16, 64, 256, 320], P('batch', 'row', 'col'), may hold values from -6 to 6
Outputs:
- input_grad: bfloat16 [16, 64, 256, 320], P('batch', 'row', 'col')
- first_kernel_grad: float32 [3, 3, 320, 320], replicated
- second_kernel_grad: float32 [3, 3, 320, 320], replicated
- norm_param_grads: float32 [4, 320], replicated
The draws below stay inside these ranges and needn't reach their ends.
All inputs are finite; a program needn't handle non-finite values.
Results may differ from the reference program's by a relative error of at most 0.002.
The reference program's roundings to bfloat16 on the way (of `act_one`, `hidden`, `act_two` and `grad_hidden`) count: a program that leaves them out, or rounds other values in their place, can miss the bound.
Values may be sent and summed in bfloat16 or wider, within the bound.
A program may use at most 128 MiB of HBM per device.

```python
import jax
import jax.numpy as jnp
from jax import lax

C = 320
GROUPS = 32
KS = 3
B = 16
H = 64
W = 256


def shard_levels(own_key, shape, shards, least, largest):
    level = 1.0
    for position, shards_of in shards:
        heights = jax.random.uniform(jax.random.fold_in(jax.random.fold_in(own_key, 6), position), (shards_of,), jnp.float32, least / len(shards), largest / len(shards))
        level = level * jnp.repeat(jnp.exp(heights), shape[position] // shards_of).reshape((-1,) + (1,) * (len(shape) - 1 - position))
    return level


def scatter_about(key, extent, width, limit, cuts=(), held_as=jnp.bfloat16):
    drawn = jax.random.normal(key, extent, jnp.float32) * width
    if len(cuts) > 0:
        drawn = shard_levels(key, extent, cuts, -0.22, 0.18) * drawn
    return jnp.clip(drawn, min=-limit, max=limit).astype(held_as)


def setup_inputs(seed: int = 0) -> dict:
    arg_keys = jax.random.split(jax.random.key(seed), 9)
    return {
        "features": scatter_about(arg_keys[0], (B, H, W, C), 1.0, 6.0, ((0, 16), (1, 4), (2, 2))),
        "first_kernel": scatter_about(arg_keys[1], (KS, KS, C, C), (KS * KS * C) ** -0.5, 0.109375),
        "second_kernel": scatter_about(arg_keys[2], (KS, KS, C, C), (KS * KS * C) ** -0.5, 0.109375),
        "first_gain": jnp.clip(1.0 + 0.1 * jax.random.normal(arg_keys[3], (C,), jnp.float32), 0.5, 1.5),
        "first_shift": scatter_about(arg_keys[4], (C,), 0.5, 3.0, (), jnp.float32),
        "second_gain": jnp.clip(1.0 + 0.1 * jax.random.normal(arg_keys[5], (C,), jnp.float32), 0.5, 1.5),
        "second_shift": scatter_about(arg_keys[6], (C,), 0.5, 3.0, (), jnp.float32),
        "upstream": scatter_about(arg_keys[7], (B, H, W, C), 1.0, 6.0, ((0, 16), (1, 4), (2, 2))),
    }


EPS = 1e-05
HIGH = lax.Precision.HIGHEST

def conv_same(values, kernel):
    return lax.conv_general_dilated(values.astype(jnp.float32), kernel.astype(jnp.float32), (1, 1), ((1, 1), (1, 1)), dimension_numbers=('NHWC', 'HWIO', 'NHWC'), precision=HIGH)

def flipped(kernel):
    return jnp.transpose(jnp.flip(kernel, (0, 1)), (0, 1, 3, 2))

def kernel_grad(values, gradient):
    padded = jnp.pad(values.astype(jnp.float32), ((0, 0), (1, 1), (1, 1), (0, 0)))
    height, breadth, chans = (gradient.shape[1], gradient.shape[2], gradient.shape[3])
    flat_grad = gradient.astype(jnp.float32).reshape(-1, chans)
    pieces = []
    for offset in range(9):
        across, along = (offset // 3, offset % 3)
        window = padded[:, across:across + height, along:along + breadth, :].reshape(-1, values.shape[3])
        pieces.append(lax.dot_general(window, flat_grad, (((0,), (0,)), ((), ())), precision=HIGH))
    return jnp.stack(pieces).reshape(3, 3, values.shape[3], chans)

def moments(values):
    bsize, chans = (values.shape[0], values.shape[3])
    grouped = values.reshape(bsize, -1, GROUPS, chans // GROUPS)
    center = lax.optimization_barrier(jnp.mean(grouped, axis=(1, 3), keepdims=True))
    shifted = grouped - center
    spread = lax.optimization_barrier(jnp.mean(shifted * shifted, axis=(1, 3), keepdims=True))
    rstd = lax.rsqrt(spread + EPS)
    return ((shifted * rstd).reshape(values.shape), rstd)

def silu_grad(grad_act, pre):
    sigma = jax.nn.sigmoid(pre)
    return grad_act * sigma * (1.0 + pre * (1.0 - sigma))

def norm_back(grad_pre, normal, rstd, gain):
    bsize, chans = (grad_pre.shape[0], grad_pre.shape[3])
    count = grad_pre.shape[1] * grad_pre.shape[2] * (chans // GROUPS)
    shift_sum = lax.optimization_barrier(jnp.sum(grad_pre, axis=(1, 2)))
    gain_sum = lax.optimization_barrier(jnp.sum(grad_pre * normal, axis=(1, 2)))
    mean_one = lax.optimization_barrier(jnp.sum((shift_sum * gain).reshape(bsize, GROUPS, -1), axis=2)) / count
    mean_two = lax.optimization_barrier(jnp.sum((gain_sum * gain).reshape(bsize, GROUPS, -1), axis=2)) / count
    scaled = (grad_pre * gain).reshape(bsize, -1, GROUPS, chans // GROUPS)
    normal_grouped = normal.reshape(scaled.shape)
    grad_in = rstd * (scaled - mean_one[:, None, :, None] - normal_grouped * mean_two[:, None, :, None])
    return (grad_in.reshape(grad_pre.shape), lax.optimization_barrier(jnp.sum(gain_sum, axis=0)), lax.optimization_barrier(jnp.sum(shift_sum, axis=0)))

def reference(features, first_kernel, second_kernel, first_gain, first_shift, second_gain, second_shift, upstream):
    normal_one, rstd_one = moments(features.astype(jnp.float32))
    pre_one = normal_one * first_gain + first_shift
    act_one = jax.nn.silu(pre_one).astype(jnp.bfloat16)
    hidden = conv_same(act_one, first_kernel).astype(jnp.bfloat16)
    normal_two, rstd_two = moments(hidden.astype(jnp.float32))
    pre_two = normal_two * second_gain + second_shift
    act_two = jax.nn.silu(pre_two).astype(jnp.bfloat16)
    second_kernel_grad = kernel_grad(act_two, upstream)
    grad_pre_two = silu_grad(conv_same(upstream, flipped(second_kernel)), pre_two)
    grad_hidden, gain_two, shift_two = norm_back(grad_pre_two, normal_two, rstd_two, second_gain)
    grad_hidden = grad_hidden.astype(jnp.bfloat16)
    first_kernel_grad = kernel_grad(act_one, grad_hidden)
    grad_pre_one = silu_grad(conv_same(grad_hidden, flipped(first_kernel)), pre_one)
    grad_input, gain_one, shift_one = norm_back(grad_pre_one, normal_one, rstd_one, first_gain)
    input_grad = (upstream.astype(jnp.float32) + grad_input).astype(jnp.bfloat16)
    norm_param_grads = jnp.stack([gain_one, shift_one, gain_two, shift_two])
    return (input_grad, first_kernel_grad, second_kernel_grad, norm_param_grads)
```

```python
import jax
import jax.numpy as jnp
from jax import lax
from jax.experimental import pallas as pl
from jax.experimental.pallas import tpu as pltpu
from jax.sharding import PartitionSpec as P

GROUPS = 32
EPS = 1e-05
R, W, C, CP = 16, 128, 320, 384
PX = R * W
PK = 1024
CHUNK = 32
COUNT = float(64 * 256 * (C // GROUPS))
F32, BF16 = jnp.float32, jnp.bfloat16
MESH = pl.DeviceIdType.MESH


def widened(v):
    return jnp.concatenate([v, jnp.zeros((v.shape[0], CP - C), v.dtype)], axis=1)


def pack3(x0, x1, x2):
    t0, t1, t2 = (x[:, 256:384] for x in (x0, x1, x2))
    low = lax.broadcasted_iota(jnp.int32, t0.shape, 1) < 64
    mid = jnp.where(low, t0, pltpu.roll(t1, 64, 1))
    end = jnp.where(low, t2, 0.0)
    return jnp.concatenate([x0[:, :256], x1[:, :256], x2[:, :256], mid, end], axis=1)


def pack_weights(k_ref, dst_ref, block):
    for i in range(3):
        for s in range(5):
            parts = []
            for j in range(3):
                a, c = block(i, j)
                parts.append(widened(k_ref[a, c, 64 * s : 64 * s + 64, :].astype(F32)))
            start = i * 256 + 64 * s if s < 4 else 768 + 64 * i
            dst_ref[start : start + 64, :] = pack3(*parts).astype(BF16)
    dst_ref[960:1024, :] = jnp.zeros((64, PK), BF16)


def fold(x):
    return jnp.sum(x.reshape(-1, 8, CP), axis=0)


def whole_sum(acc):
    return jnp.sum(acc, axis=0, keepdims=True)


def sigmoid(v):
    return 1.0 / (1.0 + jnp.exp(-v))


def kernel(
    f_hbm, k1_hbm, k2_hbm, u_hbm, par_ref,
    out_hbm, g1_hbm, g2_hbm, pg_ref,
    fb, ub, gh, k1, k2, w1, b1, b2, pad, x3, u3, y, gact, hid, act2, a1t, a2t, g, gout,
    edge32, edge, rowbuf, colbuf, stat, statbuf,
    in_sem, out_sem, hs_sem, hr_sem, ss_sem, sr_sem,
):
    row, col = lax.axis_index("row"), lax.axis_index("col")
    me = row * 2 + col

    loads = [
        pltpu.make_async_copy(src, dst, in_sem.at[n])
        for n, (src, dst) in enumerate(((f_hbm.at[0], fb), (u_hbm.at[0], ub), (k1_hbm, k1), (k2_hbm, k2)))
    ]
    for copy in loads:
        copy.start()

    def peer(d):
        other = lax.rem(me + d, 8)
        return {"row": other // 2, "col": lax.rem(other, 2)}

    barrier = pltpu.get_barrier_semaphore()
    for d in range(1, 8):
        pl.semaphore_signal(barrier, inc=1, device_id=peer(d), device_id_type=MESH)
    pl.semaphore_wait(barrier, 7)

    def stats_send(phase, first, second):
        stat[phase] = jnp.concatenate([first, second, jnp.zeros((6, CP), F32)], axis=0)
        copies = []
        for d in range(1, 8):
            copy = pltpu.make_async_remote_copy(
                stat.at[phase], statbuf.at[phase, d - 1],
                ss_sem.at[phase, d - 1], sr_sem.at[phase, d - 1],
                device_id=peer(d), device_id_type=MESH,
            )
            copy.start()
            copies.append(copy)
        return copies

    def stats_get(phase, copies):
        for copy in copies:
            copy.wait()
        total = stat[phase]
        for d in range(7):
            total = total + statbuf[phase, d]
        return total

    gi = lax.broadcasted_iota(jnp.int32, (CP, CP), 0)
    gj = lax.broadcasted_iota(jnp.int32, (CP, CP), 1)
    same = ((gi * 6554) >> 16 == (gj * 6554) >> 16) & (gi < C) & (gj < C)
    member = jnp.where(same, 1.0, 0.0).astype(F32)

    def group_means(rows):
        return jnp.dot(rows, member, precision=lax.Precision.HIGHEST, preferred_element_type=F32) / COUNT

    def norm_stats(total):
        means = group_means(total)
        mean = means[0:1]
        rstd = lax.rsqrt(means[1:2] - mean * mean + EPS)
        return mean, rstd

    up, down = lax.rem(row + 3, 4), lax.rem(row + 1, 4)
    across = 1 - col

    def halo_send(phase, src):
        edge[phase] = edge32[...].astype(BF16)
        moves = (
            (src.at[0], rowbuf.at[phase, 1], up, col),
            (src.at[R - 1], rowbuf.at[phase, 0], down, col),
            (edge.at[phase], colbuf.at[phase, 0], down, across),
            (edge.at[phase], colbuf.at[phase, 1], row, across),
            (edge.at[phase], colbuf.at[phase, 2], up, across),
        )
        copies = []
        for n, (a, b, r, c) in enumerate(moves):
            copy = pltpu.make_async_remote_copy(
                a, b, hs_sem.at[phase, n], hr_sem.at[phase, n],
                device_id={"row": r, "col": c}, device_id_type=MESH,
            )
            copy.start()
            copies.append(copy)
        return copies

    def take_edge(r, x):
        edge32[pl.ds(r, 1), :] = jnp.where(col == 0, x[W - 1 : W], x[0:1])

    def halo_fill(phase, fn):
        above, below = row > 0, row < 3
        for n, slot, ok in ((0, 0, above), (1, R + 1, below)):
            v = fn(widened(rowbuf[phase, n].astype(F32)))
            pad[slot, 8 : 8 + W, :] = jnp.where(ok, v, 0.0)
        v0 = jnp.where(above, fn(colbuf[phase, 0].astype(F32)), 0.0)
        v1 = fn(colbuf[phase, 1].astype(F32))
        v2 = jnp.where(below, fn(colbuf[phase, 2].astype(F32)), 0.0)
        for slot in range(R + 2):
            line = v0[R - 1 : R] if slot == 0 else v2[0:1] if slot == R + 1 else v1[slot - 1 : slot]
            pad[slot, 7:8, :] = jnp.where(col == 1, line, 0.0)
            pad[slot, 8 + W : 9 + W, :] = jnp.where(col == 0, line, 0.0)

    def build(dst):
        @pl.loop(0, R + 2)
        def _(s):
            dst[pl.ds(pl.multiple_of(s * W, W), W), :] = pack3(
                pad[s, 7 : 7 + W, :], pad[s, 8 : 8 + W, :], pad[s, 9 : 9 + W, :]
            ).astype(BF16)

    def conv(src, weights, transposed):
        dims = (((1,), (1 if transposed else 0,)), ((), ()))

        @pl.loop(0, 6)
        def _(s):
            rows = pl.ds(pl.multiple_of(s * 384, 384), 384)
            y[rows, :] = lax.dot_general(src[rows, :], weights[...], dims, preferred_element_type=F32)

    def combined(p, size):
        r0 = pl.ds(p, size)
        r1 = pl.ds(p + W, size)
        r2 = pl.ds(p + 2 * W, size)
        main = y[r0, 0:256] + y[r1, 256:512] + y[r2, 512:768]
        tail = y[r0, 768:896] + pltpu.roll(y[r1, 768:896], 64, 1) + y[r2, 896:1024]
        low = lax.broadcasted_iota(jnp.int32, tail.shape, 1) < 64
        return jnp.concatenate([main, jnp.where(low, tail, 0.0)], axis=1)

    def chunks(body, init):
        def step(n, carry):
            return body(pl.multiple_of(n * CHUNK, CHUNK), carry)

        return lax.fori_loop(0, PX // CHUNK, step, init)

    def kernel_grad(left, right):
        @pl.loop(0, 12)
        def _(n):
            a, part = n // 4, lax.rem(n, 4)
            rows = pl.ds(pl.multiple_of((2 - a) * W, W), PX)
            cols = pl.ds(pl.multiple_of(part * 256, 256), 256)
            g[a, :, cols] = jnp.dot(left[...], right[rows, cols], preferred_element_type=F32)

    def kernel_grad_out(hbm, sem):
        for a in range(3):
            for c in range(3):
                b = 2 - c
                gout[a, c, :, 0:256] = g[a, :, b * 256 : b * 256 + 256]
                t = g[a, :, 896:1024] if b == 2 else g[a, :, 768:896]
                if b == 1:
                    t = pltpu.roll(t, 64, 1)
                gout[a, c, :, 256:320] = t[:, 0:64]
        copy = pltpu.make_async_copy(gout, hbm, sem)
        copy.start()
        return copy

    zero = jnp.zeros((8, CP), F32)
    g1, s1, g2, s2 = (par_ref[n : n + 1, :] for n in range(4))

    loads[0].wait()

    def first_stats(r, carry):
        total, square = carry
        x = widened(fb[r].astype(F32))
        take_edge(r, x)
        return total + fold(x), square + fold(x * x)

    total, square = lax.fori_loop(0, R, first_stats, (zero, zero))
    sent_one = stats_send(0, whole_sum(total), whole_sum(square))
    halo_one = halo_send(0, fb)

    loads[1].wait()

    @pl.loop(0, R)
    def _(r):
        x = widened(ub[r].astype(F32))
        take_edge(r, x)
        pad[r + 1, 8 : 8 + W, :] = x

    halo_up = halo_send(1, ub)
    loads[2].wait()
    pack_weights(k1, w1, lambda i, j: (j, i))
    loads[3].wait()
    pack_weights(k2, b2, lambda i, j: (2 - i, 2 - j))
    for copy in halo_up:
        copy.wait()
    halo_fill(1, lambda v: v)
    build(u3)

    mean1, rstd1 = norm_stats(stats_get(0, sent_one))
    for copy in halo_one:
        copy.wait()

    def act_one(x):
        v = (x - mean1) * rstd1 * g1 + s1
        return (v * sigmoid(v)).astype(BF16).astype(F32)

    @pl.loop(0, R * 4)
    def _(n):
        r, q = n // 4, lax.rem(n, 4)
        p = pl.multiple_of(q * CHUNK, CHUNK)
        pad[r + 1, pl.ds(8 + p, CHUNK), :] = act_one(widened(fb[r, pl.ds(p, CHUNK), :].astype(F32)))

    halo_fill(0, act_one)
    build(x3)
    conv(x3, w1, False)

    def hidden_stats(p, carry):
        total, square = carry
        h = combined(p, CHUNK).astype(BF16)
        hid[pl.ds(p, CHUNK), :] = h
        h = h.astype(F32)
        return total + fold(h), square + fold(h * h)

    total, square = chunks(hidden_stats, (zero, zero))
    sent_two = stats_send(1, whole_sum(total), whole_sum(square))

    conv(u3, b2, True)

    @pl.loop(0, R)
    def _(r):
        where = pl.ds(pl.multiple_of(r * W, W), W)
        a1t[:, where] = pad[r + 1, 8 : 8 + W, :].T[:C].astype(BF16)

    mean2, rstd2 = norm_stats(stats_get(1, sent_two))

    def second_back(p, carry):
        shift, gain = carry
        here = pl.ds(p, CHUNK)
        n2 = (hid[here, :].astype(F32) - mean2) * rstd2
        pre = n2 * g2 + s2
        s = sigmoid(pre)
        act2[here, :] = pre * s
        gp = combined(p, CHUNK) * s * (1.0 + pre * (1.0 - s))
        gact[here, :] = gp
        return shift + fold(gp), gain + fold(gp * n2)

    shift, gain = chunks(second_back, (zero, zero))
    shift2, gain2 = whole_sum(shift), whole_sum(gain)
    sent_three = stats_send(2, shift2, gain2)

    @pl.loop(0, R)
    def _(r):
        where = pl.ds(pl.multiple_of(r * W, W), W)
        a2t[:, where] = act2[where, :].T[:C].astype(BF16)

    kernel_grad(a2t, u3)
    out_two = kernel_grad_out(g2_hbm, out_sem.at[0])

    means = group_means(stats_get(2, sent_three) * g2)
    m1, m2 = means[0:1], means[1:2]

    @pl.loop(0, R)
    def _(r):
        for q in range(W // CHUNK):
            here = pl.ds(pl.multiple_of(r * W + q * CHUNK, CHUNK), CHUNK)
            n2 = (hid[here, :].astype(F32) - mean2) * rstd2
            v = rstd2 * (gact[here, :] * g2 - m1 - n2 * m2)
            v = v.astype(BF16)
            gh[r, q * CHUNK : q * CHUNK + CHUNK, :] = v[:, :C]
            pad[r + 1, 8 + q * CHUNK : 8 + q * CHUNK + CHUNK, :] = v.astype(F32)
        edge32[pl.ds(r, 1), :] = jnp.where(
            col == 0, pad[r + 1, 7 + W : 8 + W, :], pad[r + 1, 8:9, :]
        )

    halo_gh = halo_send(2, gh)
    pack_weights(k1, b1, lambda i, j: (2 - i, 2 - j))
    for copy in halo_gh:
        copy.wait()
    halo_fill(2, lambda v: v)
    build(x3)
    kernel_grad(a1t, x3)
    out_two.wait()
    out_one = kernel_grad_out(g1_hbm, out_sem.at[1])
    conv(x3, b1, True)

    def norm_one(r, p):
        return (widened(fb[r, pl.ds(p, CHUNK), :].astype(F32)) - mean1) * rstd1

    def first_back(n, carry):
        shift, gain = carry
        r, q = n // 4, lax.rem(n, 4)
        p = pl.multiple_of(n * CHUNK, CHUNK)
        n1 = norm_one(r, pl.multiple_of(q * CHUNK, CHUNK))
        pre = n1 * g1 + s1
        s = sigmoid(pre)
        gp = combined(p, CHUNK) * s * (1.0 + pre * (1.0 - s))
        gact[pl.ds(p, CHUNK), :] = gp
        return shift + fold(gp), gain + fold(gp * n1)

    shift, gain = lax.fori_loop(0, PX // CHUNK, first_back, (zero, zero))
    shift1, gain1 = whole_sum(shift), whole_sum(gain)
    sent_four = stats_send(3, shift1, gain1)
    pg_ref[...] = jnp.concatenate([gain1, shift1, gain2, shift2, jnp.zeros((4, CP), F32)], axis=0)
    means = group_means(stats_get(3, sent_four) * g1)
    n_one, n_two = means[0:1], means[1:2]

    @pl.loop(0, PX // CHUNK)
    def _(n):
        r, q = n // 4, lax.rem(n, 4)
        p = pl.multiple_of(q * CHUNK, CHUNK)
        n1 = norm_one(r, p)
        v = rstd1 * (gact[pl.ds(pl.multiple_of(n * CHUNK, CHUNK), CHUNK), :] * g1 - n_one - n1 * n_two)
        gh[r, pl.ds(p, CHUNK), :] = (ub[r, pl.ds(p, CHUNK), :].astype(F32) + v[:, :C]).astype(BF16)

    out_main = pltpu.make_async_copy(gh, out_hbm.at[0], out_sem.at[2])
    out_main.start()
    out_one.wait()
    out_main.wait()


def per_device(features, first_kernel, second_kernel, first_gain, first_shift, second_gain, second_shift, upstream):
    params = jnp.pad(jnp.stack([first_gain, first_shift, second_gain, second_shift]), ((0, 4), (0, CP - C)))
    hbm = pl.BlockSpec(memory_space=pl.ANY)
    vmem = pl.BlockSpec(memory_space=pltpu.VMEM)
    grad = jax.ShapeDtypeStruct((3, 3, C, C), F32)
    input_grad, g1, g2, pg = pl.pallas_call(
        kernel,
        out_shape=(jax.ShapeDtypeStruct((1, R, W, C), BF16), grad, grad, jax.ShapeDtypeStruct((8, CP), F32)),
        in_specs=[hbm, hbm, hbm, hbm, vmem],
        out_specs=(hbm, hbm, hbm, vmem),
        scratch_shapes=[
            pltpu.VMEM((R, W, C), BF16),
            pltpu.VMEM((R, W, C), BF16),
            pltpu.VMEM((R, W, C), BF16),
            pltpu.VMEM((3, 3, C, C), BF16),
            pltpu.VMEM((3, 3, C, C), BF16),
            pltpu.VMEM((PK, PK), BF16),
            pltpu.VMEM((PK, PK), BF16),
            pltpu.VMEM((PK, PK), BF16),
            pltpu.VMEM((R + 2, W + 16, CP), F32),
            pltpu.VMEM(((R + 2) * W, PK), BF16),
            pltpu.VMEM(((R + 2) * W, PK), BF16),
            pltpu.VMEM(((R + 2) * W, PK), F32),
            pltpu.VMEM((PX, CP), F32),
            pltpu.VMEM((PX, CP), BF16),
            pltpu.VMEM((PX, CP), F32),
            pltpu.VMEM((C, PX), BF16),
            pltpu.VMEM((C, PX), BF16),
            pltpu.VMEM((3, C, PK), F32),
            pltpu.VMEM((3, 3, C, C), F32),
            pltpu.VMEM((R, CP), F32),
            pltpu.VMEM((3, R, CP), BF16),
            pltpu.VMEM((3, 2, W, C), BF16),
            pltpu.VMEM((3, 3, R, CP), BF16),
            pltpu.VMEM((4, 8, CP), F32),
            pltpu.VMEM((4, 7, 8, CP), F32),
            pltpu.SemaphoreType.DMA((4,)),
            pltpu.SemaphoreType.DMA((3,)),
            pltpu.SemaphoreType.DMA((3, 5)),
            pltpu.SemaphoreType.DMA((3, 5)),
            pltpu.SemaphoreType.DMA((4, 7)),
            pltpu.SemaphoreType.DMA((4, 7)),
        ],
        compiler_params=pltpu.CompilerParams(
            collective_id=0, has_side_effects=True, vmem_limit_bytes=67_000_000
        ),
        name="resblock_backward",
    )(features, first_kernel, second_kernel, upstream, params)
    g1, g2, pg = lax.psum((g1, g2, pg[:4, :C]), ("batch", "row", "col"))
    return input_grad, g1, g2, pg


def solution(mesh):
    tiles = P("batch", "row", "col", None)
    return jax.shard_map(
        per_device,
        mesh=mesh,
        in_specs=(tiles, P(), P(), P(), P(), P(), P(), tiles),
        out_specs=(tiles, P(), P(), P()),
        check_vma=False,
    )
```

```python
import jax
import jax.numpy as jnp
from jax import lax
from jax.experimental import pallas as pl
from jax.experimental.pallas import tpu as pltpu
from jax.sharding import PartitionSpec as P

GROUPS = 32
EPS = 1e-05
R, W, C, CP = 16, 128, 320, 384
PX = R * W
PK = 1024
CHUNK = 32
COUNT = float(64 * 256 * (C // GROUPS))
F32, BF16 = jnp.float32, jnp.bfloat16
MESH = pl.DeviceIdType.MESH


def widened(v):
    return jnp.concatenate([v, jnp.zeros((v.shape[0], CP - C), v.dtype)], axis=1)


def pack3(x0, x1, x2):
    t0, t1, t2 = (x[:, 256:384] for x in (x0, x1, x2))
    low = lax.broadcasted_iota(jnp.int32, t0.shape, 1) < 64
    mid = jnp.where(low, t0, pltpu.roll(t1, 64, 1))
    end = jnp.where(low, t2, 0.0)
    return jnp.concatenate([x0[:, :256], x1[:, :256], x2[:, :256], mid, end], axis=1)


def pack_weights(k_ref, dst_ref, block):
    for i in range(3):
        for s in range(5):
            parts = []
            for j in range(3):
                a, c = block(i, j)
                parts.append(widened(k_ref[a, c, 64 * s : 64 * s + 64, :].astype(F32)))
            start = i * 256 + 64 * s if s < 4 else 768 + 64 * i
            dst_ref[start : start + 64, :] = pack3(*parts).astype(BF16)
    dst_ref[960:1024, :] = jnp.zeros((64, PK), BF16)


def fold(x):
    return jnp.sum(x.reshape(-1, 8, CP), axis=0)


def whole_sum(acc):
    return jnp.sum(acc, axis=0, keepdims=True)


def sigmoid(v):
    return 1.0 / (1.0 + jnp.exp(-v))


def kernel(
    f_hbm, k1_hbm, k2_hbm, u_hbm, par_ref,
    out_hbm, g_hbm, pg_ref,
    fb, ub, gh, k1, k2, w1, b2, pad, x3, u3, y, gact, hid, a1t, a2t, gs,
    cbuf, s1buf, s2buf, s3buf, edge32, edge, rowbuf, colbuf, statbuf, pgbuf,
    in_sem, out_sem, hs_sem, hr_sem, ss_sem, sr_sem, ps_sem, pr_sem, rs_sem, rr_sem, free_sem,
):
    row, col, batch = lax.axis_index("row"), lax.axis_index("col"), lax.axis_index("batch")
    me = row * 2 + col
    core, near, deep = lax.rem(batch, 2), lax.rem(batch // 2, 2), batch // 4
    spot = (row, col * 2 + near, deep)
    inner = near * 2 + core

    def device(x=row, hi=col, lo=near, z=deep, side=core):
        return {"batch": (z * 2 + lo) * 2 + side, "row": x, "col": hi}

    def along(axis, d):
        j = lax.rem(spot[axis] + d, 4)
        if axis == 0:
            return j, device(x=j)
        if axis == 1:
            return j, device(hi=j // 2, lo=lax.rem(j, 2))
        return j, device(z=j)

    loads = [
        pltpu.make_async_copy(src, dst, in_sem.at[n])
        for n, (src, dst) in enumerate(((f_hbm.at[0], fb), (u_hbm.at[0], ub), (k1_hbm, k1), (k2_hbm, k2)))
    ]
    for copy in loads:
        copy.start()

    def peer(d):
        other = lax.rem(me + d, 8)
        return device(x=other // 2, hi=lax.rem(other, 2))

    barrier = pltpu.get_barrier_semaphore()
    others = [peer(d) for d in range(1, 8)] + [along(2, d)[1] for d in range(1, 4)]
    others += [device(side=1 - core), device(lo=1 - near), device(lo=1 - near, hi=1 - col)]
    others += [device(lo=1 - near, side=1 - core)]
    for other in others:
        pl.semaphore_signal(barrier, inc=1, device_id=other, device_id_type=MESH)
    pl.semaphore_wait(barrier, len(others))

    def stats_send(phase, first, second):
        statbuf[phase, me] = jnp.concatenate([first, second, jnp.zeros((6, CP), F32)], axis=0)
        copies = []
        for d in range(1, 8):
            copy = pltpu.make_async_remote_copy(
                statbuf.at[phase, me], statbuf.at[phase, me],
                ss_sem.at[phase, d - 1], sr_sem.at[phase, d - 1],
                device_id=peer(d), device_id_type=MESH,
            )
            copy.start()
            copies.append(copy)
        return copies

    def stats_get(phase, copies):
        for copy in copies:
            copy.wait()
        total = statbuf[phase, 0]
        for n in range(1, 8):
            total = total + statbuf[phase, n]
        return total

    def send(sems, index, src, dst, target):
        copy = pltpu.make_async_remote_copy(
            src, dst, sems[0].at[index], sems[1].at[index], device_id=target, device_id_type=MESH
        )
        copy.start()
        return copy

    def wait_all(copies):
        for copy in copies:
            copy.wait()

    mine = pl.ds(pl.multiple_of(core * 160, 8), 160)
    theirs = pl.ds(pl.multiple_of((1 - core) * 160, 8), 160)

    def forty(j):
        return pl.ds(pl.multiple_of(core * 160 + j * 40, 8), 40)

    def quarter(j):
        return pl.ds(pl.multiple_of(j * 256, 256), 256)

    def pair_send(t, a):
        return send(
            (rs_sem, rr_sem), (t, 0, a, 0), gs.at[t, a, theirs, :], cbuf.at[t, a], device(side=1 - core)
        )

    def reduce_steps(t, pair):
        sems = (rs_sem, rr_sem)
        axes = [[(a + n) % 3 for n in range(3)] for a in range(3)]
        rows = [forty(spot[axes[a][0]]) for a in range(3)]
        cols = [quarter(spot[axes[a][1]]) for a in range(3)]
        flying = [[], [], []]

        def sent(stage, a, targets):
            for target in targets:
                pl.semaphore_signal(free_sem.at[t, stage, a], inc=1, device_id=target, device_id_type=MESH)

        def ring(a, n):
            return [along(axes[a][n], d)[1] for d in range(1, 4)]

        for a in range(3):
            pair[a].wait()
            sent(0, a, [device(side=1 - core)])
            gs[t, a, mine, :] += cbuf[t, a]
            for d in range(1, 4):
                j, target = along(axes[a][0], d)
                flying[a].append(
                    send(sems, (t, 1, a, d - 1), gs.at[t, a, forty(j), :], s1buf.at[t, a, d - 1], target)
                )
        yield
        for a in range(3):
            wait_all(flying[a])
            sent(1, a, ring(a, 0))
            gs[t, a, rows[a], :] += s1buf[t, a, 0] + s1buf[t, a, 1] + s1buf[t, a, 2]
            flying[a] = []
            for d in range(1, 4):
                j, target = along(axes[a][1], d)
                flying[a].append(
                    send(sems, (t, 2, a, d - 1), gs.at[t, a, rows[a], quarter(j)], s2buf.at[t, a, d - 1], target)
                )
        yield
        for a in range(3):
            wait_all(flying[a])
            sent(2, a, ring(a, 1))
            slot = spot[axes[a][2]]
            s3buf[t, a, slot] = gs[t, a, rows[a], cols[a]] + (s2buf[t, a, 0] + s2buf[t, a, 1] + s2buf[t, a, 2])
            flying[a] = []
            for d in range(1, 4):
                _, target = along(axes[a][2], d)
                flying[a].append(
                    send(sems, (t, 3, a, d - 1), s3buf.at[t, a, slot], s3buf.at[t, a, slot], target)
                )
        yield
        for a in range(3):
            wait_all(flying[a])
            gs[t, a, rows[a], cols[a]] = (s3buf[t, a, 0] + s3buf[t, a, 1]) + (s3buf[t, a, 2] + s3buf[t, a, 3])
            block = gs.at[t, a, rows[a], cols[a]]
            pl.semaphore_wait(free_sem.at[t, 2, a], 3)
            flying[a] = [
                send(sems, (t, 4, a, d - 1), block, block, along(axes[a][1], d)[1]) for d in range(1, 4)
            ]
        yield
        for a in range(3):
            wait_all(flying[a])
            block = gs.at[t, a, rows[a], :]
            pl.semaphore_wait(free_sem.at[t, 1, a], 3)
            flying[a] = [
                send(sems, (t, 5, a, d - 1), block, block, along(axes[a][0], d)[1]) for d in range(1, 4)
            ]
        yield
        for a in range(3):
            wait_all(flying[a])
            block = gs.at[t, a, mine, :]
            pl.semaphore_wait(free_sem.at[t, 0, a], 1)
            flying[a] = [send(sems, (t, 6, a, 0), block, block, device(side=1 - core))]
        yield
        for a in range(3):
            wait_all(flying[a])
        copy = pltpu.make_async_copy(gs.at[t], g_hbm.at[t], out_sem.at[t])
        copy.start()
        yield copy

    def param_steps(value):
        slots = (deep, inner)
        for n in range(2):
            slot = slots[n]
            pgbuf[n, slot] = value
            flying = []
            for d in range(1, 4):
                j = lax.rem(slot + d, 4)
                target = device(z=j) if n == 0 else device(lo=j // 2, side=lax.rem(j, 2))
                flying.append(send((ps_sem, pr_sem), (n, d - 1), pgbuf.at[n, slot], pgbuf.at[n, slot], target))
            yield
            wait_all(flying)
            value = (pgbuf[n, 0] + pgbuf[n, 1]) + (pgbuf[n, 2] + pgbuf[n, 3])
        pg_ref[...] = value
        yield

    gi = lax.broadcasted_iota(jnp.int32, (CP, CP), 0)
    gj = lax.broadcasted_iota(jnp.int32, (CP, CP), 1)
    same = ((gi * 6554) >> 16 == (gj * 6554) >> 16) & (gi < C) & (gj < C)
    member = jnp.where(same, 1.0, 0.0).astype(F32)

    def group_means(rows):
        return jnp.dot(rows, member, precision=lax.Precision.HIGHEST, preferred_element_type=F32) / COUNT

    def norm_stats(total):
        means = group_means(total)
        mean = means[0:1]
        rstd = lax.rsqrt(means[1:2] - mean * mean + EPS)
        return mean, rstd

    up, down = lax.rem(row + 3, 4), lax.rem(row + 1, 4)
    across = 1 - col

    def halo_send(phase, src):
        edge[phase] = edge32[...].astype(BF16)
        moves = (
            (src.at[0], rowbuf.at[phase, 1], up, col),
            (src.at[R - 1], rowbuf.at[phase, 0], down, col),
            (edge.at[phase], colbuf.at[phase, 0], down, across),
            (edge.at[phase], colbuf.at[phase, 1], row, across),
            (edge.at[phase], colbuf.at[phase, 2], up, across),
        )
        copies = []
        for n, (a, b, r, c) in enumerate(moves):
            copy = pltpu.make_async_remote_copy(
                a, b, hs_sem.at[phase, n], hr_sem.at[phase, n],
                device_id=device(x=r, hi=c), device_id_type=MESH,
            )
            copy.start()
            copies.append(copy)
        return copies

    def take_edge(r, x):
        edge32[pl.ds(r, 1), :] = jnp.where(col == 0, x[W - 1 : W], x[0:1])

    def halo_fill(phase, fn):
        above, below = row > 0, row < 3
        for n, slot, ok in ((0, 0, above), (1, R + 1, below)):
            v = fn(widened(rowbuf[phase, n].astype(F32)))
            pad[slot, 8 : 8 + W, :] = jnp.where(ok, v, 0.0)
        v0 = jnp.where(above, fn(colbuf[phase, 0].astype(F32)), 0.0)
        v1 = fn(colbuf[phase, 1].astype(F32))
        v2 = jnp.where(below, fn(colbuf[phase, 2].astype(F32)), 0.0)
        for slot in range(R + 2):
            line = v0[R - 1 : R] if slot == 0 else v2[0:1] if slot == R + 1 else v1[slot - 1 : slot]
            pad[slot, 7:8, :] = jnp.where(col == 1, line, 0.0)
            pad[slot, 8 + W : 9 + W, :] = jnp.where(col == 0, line, 0.0)

    def build(dst):
        @pl.loop(0, R + 2)
        def _(s):
            dst[pl.ds(pl.multiple_of(s * W, W), W), :] = pack3(
                pad[s, 7 : 7 + W, :], pad[s, 8 : 8 + W, :], pad[s, 9 : 9 + W, :]
            ).astype(BF16)

    def conv(src, weights, transposed):
        dims = (((1,), (1 if transposed else 0,)), ((), ()))

        @pl.loop(0, 6)
        def _(s):
            rows = pl.ds(pl.multiple_of(s * 384, 384), 384)
            y[rows, :] = lax.dot_general(src[rows, :], weights[...], dims, preferred_element_type=F32)

    def combined(p, size):
        r0 = pl.ds(p, size)
        r1 = pl.ds(p + W, size)
        r2 = pl.ds(p + 2 * W, size)
        main = y[r0, 0:256] + y[r1, 256:512] + y[r2, 512:768]
        tail = y[r0, 768:896] + pltpu.roll(y[r1, 768:896], 64, 1) + y[r2, 896:1024]
        low = lax.broadcasted_iota(jnp.int32, tail.shape, 1) < 64
        return jnp.concatenate([main, jnp.where(low, tail, 0.0)], axis=1)

    def chunks(body, init):
        def step(n, carry):
            return body(pl.multiple_of(n * CHUNK, CHUNK), carry)

        return lax.fori_loop(0, PX // CHUNK, step, init)

    def kernel_grad(left, right, t):
        pair = []
        for a in range(3):
            rows = pl.ds((2 - a) * W, PX)

            @pl.loop(0, 4)
            def _(part):
                cols = pl.ds(pl.multiple_of(part * 256, 256), 256)
                gs[t, a, :, cols] = jnp.dot(left[...], right[rows, cols], preferred_element_type=F32)

            pair.append(pair_send(t, a))
        return pair

    zero = jnp.zeros((8, CP), F32)
    g1, s1, g2, s2 = (par_ref[n : n + 1, :] for n in range(4))

    loads[0].wait()

    def first_stats(r, carry):
        total, square = carry
        x = widened(fb[r].astype(F32))
        take_edge(r, x)
        return total + fold(x), square + fold(x * x)

    total, square = lax.fori_loop(0, R, first_stats, (zero, zero))
    sent_one = stats_send(0, whole_sum(total), whole_sum(square))
    halo_one = halo_send(0, fb)

    loads[1].wait()

    @pl.loop(0, R)
    def _(r):
        x = widened(ub[r].astype(F32))
        take_edge(r, x)
        pad[r + 1, 8 : 8 + W, :] = x

    halo_up = halo_send(1, ub)
    loads[2].wait()
    pack_weights(k1, w1, lambda i, j: (j, i))
    loads[3].wait()
    pack_weights(k2, b2, lambda i, j: (2 - i, 2 - j))
    for copy in halo_up:
        copy.wait()
    halo_fill(1, lambda v: v)
    build(u3)

    mean1, rstd1 = norm_stats(stats_get(0, sent_one))
    for copy in halo_one:
        copy.wait()

    def act_one(x):
        v = (x - mean1) * rstd1 * g1 + s1
        return (v * sigmoid(v)).astype(BF16).astype(F32)

    @pl.loop(0, R * 4)
    def _(n):
        r, q = n // 4, lax.rem(n, 4)
        p = pl.multiple_of(q * CHUNK, CHUNK)
        pad[r + 1, pl.ds(8 + p, CHUNK), :] = act_one(widened(fb[r, pl.ds(p, CHUNK), :].astype(F32)))

    halo_fill(0, act_one)
    build(x3)
    conv(x3, w1, False)

    def hidden_stats(p, carry):
        total, square = carry
        h = combined(p, CHUNK).astype(BF16)
        hid[pl.ds(p, CHUNK), :] = h
        h = h.astype(F32)
        return total + fold(h), square + fold(h * h)

    total, square = chunks(hidden_stats, (zero, zero))
    sent_two = stats_send(1, whole_sum(total), whole_sum(square))

    conv(u3, b2, True)

    @pl.loop(0, R)
    def _(r):
        where = pl.ds(pl.multiple_of(r * W, W), W)
        a1t[:, where] = pad[r + 1, 8 : 8 + W, :].T[:C].astype(BF16)

    mean2, rstd2 = norm_stats(stats_get(1, sent_two))

    def second_back(p, carry):
        shift, gain = carry
        here = pl.ds(p, CHUNK)
        q = pl.multiple_of(8 + lax.rem(p, W), 8)
        n2 = (hid[here, :].astype(F32) - mean2) * rstd2
        pre = n2 * g2 + s2
        s = sigmoid(pre)
        pad[p // W + 1, pl.ds(q, CHUNK), :] = pre * s
        gp = combined(p, CHUNK) * s * (1.0 + pre * (1.0 - s))
        gact[here, :] = gp
        return shift + fold(gp), gain + fold(gp * n2)

    shift, gain = chunks(second_back, (zero, zero))
    shift2, gain2 = whole_sum(shift), whole_sum(gain)
    sent_three = stats_send(2, shift2, gain2)

    @pl.loop(0, R)
    def _(r):
        where = pl.ds(pl.multiple_of(r * W, W), W)
        a2t[:, where] = pad[r + 1, 8 : 8 + W, :].T[:C].astype(BF16)

    steps2 = reduce_steps(0, kernel_grad(a2t, u3, 0))
    total2 = stats_get(2, sent_three)
    means = group_means(total2 * g2)
    m1, m2 = means[0:1], means[1:2]

    @pl.loop(0, R)
    def _(r):
        for q in range(W // CHUNK):
            here = pl.ds(pl.multiple_of(r * W + q * CHUNK, CHUNK), CHUNK)
            n2 = (hid[here, :].astype(F32) - mean2) * rstd2
            v = rstd2 * (gact[here, :] * g2 - m1 - n2 * m2)
            v = v.astype(BF16)
            gh[r, q * CHUNK : q * CHUNK + CHUNK, :] = v[:, :C]
            pad[r + 1, 8 + q * CHUNK : 8 + q * CHUNK + CHUNK, :] = v.astype(F32)
        edge32[pl.ds(r, 1), :] = jnp.where(
            col == 0, pad[r + 1, 7 + W : 8 + W, :], pad[r + 1, 8:9, :]
        )

    halo_gh = halo_send(2, gh)
    next(steps2)
    pack_weights(k1, w1, lambda i, j: (2 - i, 2 - j))
    for copy in halo_gh:
        copy.wait()
    halo_fill(2, lambda v: v)
    build(x3)
    next(steps2)
    steps1 = reduce_steps(1, kernel_grad(a1t, x3, 1))
    next(steps2)
    conv(x3, w1, True)
    next(steps2)
    next(steps1)

    def norm_one(r, p):
        return (widened(fb[r, pl.ds(p, CHUNK), :].astype(F32)) - mean1) * rstd1

    def first_back(n, carry):
        shift, gain = carry
        r, q = n // 4, lax.rem(n, 4)
        p = pl.multiple_of(n * CHUNK, CHUNK)
        n1 = norm_one(r, pl.multiple_of(q * CHUNK, CHUNK))
        pre = n1 * g1 + s1
        s = sigmoid(pre)
        gp = combined(p, CHUNK) * s * (1.0 + pre * (1.0 - s))
        gact[pl.ds(p, CHUNK), :] = gp
        return shift + fold(gp), gain + fold(gp * n1)

    shift, gain = lax.fori_loop(0, PX // CHUNK, first_back, (zero, zero))
    shift1, gain1 = whole_sum(shift), whole_sum(gain)
    sent_four = stats_send(3, shift1, gain1)
    next(steps2)
    next(steps1)
    total1 = stats_get(3, sent_four)
    means = group_means(total1 * g1)
    steps_p = param_steps(
        jnp.concatenate([total1[1:2], total1[0:1], total2[1:2], total2[0:1], jnp.zeros((4, CP), F32)], axis=0)
    )
    next(steps_p)
    next(steps2)
    next(steps1)
    n_one, n_two = means[0:1], means[1:2]

    @pl.loop(0, PX // CHUNK)
    def _(n):
        r, q = n // 4, lax.rem(n, 4)
        p = pl.multiple_of(q * CHUNK, CHUNK)
        n1 = norm_one(r, p)
        v = rstd1 * (gact[pl.ds(pl.multiple_of(n * CHUNK, CHUNK), CHUNK), :] * g1 - n_one - n1 * n_two)
        gh[r, pl.ds(p, CHUNK), :] = (ub[r, pl.ds(p, CHUNK), :].astype(F32) + v[:, :C]).astype(BF16)

    out_main = pltpu.make_async_copy(gh, out_hbm.at[0], out_sem.at[2])
    out_main.start()
    next(steps1)
    next(steps_p)
    out_two = next(steps2)
    next(steps1)
    next(steps_p)
    next(steps1)
    out_one = next(steps1)
    out_two.wait()
    out_main.wait()
    out_one.wait()


def unpack(g_ref, g1_ref, g2_ref):
    for t, dst in ((0, g2_ref), (1, g1_ref)):
        for c in range(3):
            b = 2 - c
            dst[0, c, :, 0:256] = g_ref[t, 0, :, b * 256 : b * 256 + 256]
            x = g_ref[t, 0, :, 896:1024] if b == 2 else g_ref[t, 0, :, 768:896]
            if b == 1:
                x = pltpu.roll(x, 64, 1)
            dst[0, c, :, 256:320] = x[:, 0:64]


def per_device(features, first_kernel, second_kernel, first_gain, first_shift, second_gain, second_shift, upstream):
    params = jnp.pad(jnp.stack([first_gain, first_shift, second_gain, second_shift]), ((0, 4), (0, CP - C)))
    hbm = pl.BlockSpec(memory_space=pl.ANY)
    vmem = pl.BlockSpec(memory_space=pltpu.VMEM)
    input_grad, packed, pg = pl.pallas_call(
        kernel,
        out_shape=(
            jax.ShapeDtypeStruct((1, R, W, C), BF16),
            jax.ShapeDtypeStruct((2, 3, C, PK), F32),
            jax.ShapeDtypeStruct((8, CP), F32),
        ),
        in_specs=[hbm, hbm, hbm, hbm, vmem],
        out_specs=(hbm, hbm, vmem),
        scratch_shapes=[
            pltpu.VMEM((R, W, C), BF16),
            pltpu.VMEM((R, W, C), BF16),
            pltpu.VMEM((R, W, C), BF16),
            pltpu.VMEM((3, 3, C, C), BF16),
            pltpu.VMEM((3, 3, C, C), BF16),
            pltpu.VMEM((PK, PK), BF16),
            pltpu.VMEM((PK, PK), BF16),
            pltpu.VMEM((R + 2, W + 16, CP), F32),
            pltpu.VMEM(((R + 2) * W, PK), BF16),
            pltpu.VMEM(((R + 2) * W, PK), BF16),
            pltpu.VMEM(((R + 2) * W, PK), F32),
            pltpu.VMEM((PX, CP), F32),
            pltpu.VMEM((PX, CP), BF16),
            pltpu.VMEM((C, PX), BF16),
            pltpu.VMEM((C, PX), BF16),
            pltpu.VMEM((2, 3, C, PK), F32),
            pltpu.VMEM((2, 3, 160, PK), F32),
            pltpu.VMEM((2, 3, 3, 40, PK), F32),
            pltpu.VMEM((2, 3, 3, 40, 256), F32),
            pltpu.VMEM((2, 3, 4, 40, 256), F32),
            pltpu.VMEM((R, CP), F32),
            pltpu.VMEM((3, R, CP), BF16),
            pltpu.VMEM((3, 2, W, C), BF16),
            pltpu.VMEM((3, 3, R, CP), BF16),
            pltpu.VMEM((4, 8, 8, CP), F32),
            pltpu.VMEM((2, 4, 8, CP), F32),
            pltpu.SemaphoreType.DMA((4,)),
            pltpu.SemaphoreType.DMA((3,)),
            pltpu.SemaphoreType.DMA((3, 5)),
            pltpu.SemaphoreType.DMA((3, 5)),
            pltpu.SemaphoreType.DMA((4, 7)),
            pltpu.SemaphoreType.DMA((4, 7)),
            pltpu.SemaphoreType.DMA((2, 3)),
            pltpu.SemaphoreType.DMA((2, 3)),
            pltpu.SemaphoreType.DMA((2, 7, 3, 3)),
            pltpu.SemaphoreType.DMA((2, 7, 3, 3)),
            pltpu.SemaphoreType.REGULAR((2, 3, 3)),
        ],
        compiler_params=pltpu.CompilerParams(
            collective_id=0, has_side_effects=True, vmem_limit_bytes=67_000_000
        ),
        name="resblock_backward",
    )(features, first_kernel, second_kernel, upstream, params)
    grad = jax.ShapeDtypeStruct((3, 3, C, C), F32)
    taps = pl.BlockSpec((1, 3, C, C), lambda a: (a, 0, 0, 0))
    g1, g2 = pl.pallas_call(
        unpack,
        grid=(3,),
        out_shape=(grad, grad),
        in_specs=[pl.BlockSpec((2, 1, C, PK), lambda a: (0, a, 0, 0))],
        out_specs=(taps, taps),
        name="unpack",
    )(packed)
    return input_grad, g1, g2, pg[:4, :C]


def solution(mesh):
    tiles = P("batch", "row", "col", None)
    return jax.shard_map(
        per_device,
        mesh=mesh,
        in_specs=(tiles, P(), P(), P(), P(), P(), P(), tiles),
        out_specs=(tiles, P(), P(), P()),
        check_vma=False,
    )
```

```python
import jax
import jax.numpy as jnp
from jax import lax
from jax.experimental import pallas as pl
from jax.experimental.pallas import tpu as pltpu
from jax.sharding import PartitionSpec as P

GROUPS = 32
EPS = 1e-05
R, W, C, CP = 16, 128, 320, 384
PX = R * W
PK = 1024
CHUNK = 32
COUNT = float(64 * 256 * (C // GROUPS))
F32, BF16 = jnp.float32, jnp.bfloat16
MESH = pl.DeviceIdType.MESH


def widened(v):
    return jnp.concatenate([v, jnp.zeros((v.shape[0], CP - C), v.dtype)], axis=1)


def pack3(x0, x1, x2):
    t0, t1, t2 = (x[:, 256:384] for x in (x0, x1, x2))
    low = lax.broadcasted_iota(jnp.int32, t0.shape, 1) < 64
    mid = jnp.where(low, t0, pltpu.roll(t1, 64, 1))
    end = jnp.where(low, t2, 0.0)
    return jnp.concatenate([x0[:, :256], x1[:, :256], x2[:, :256], mid, end], axis=1)


def pack_weights(k_ref, dst_ref, block):
    for i in range(3):
        for s in range(5):
            parts = []
            for j in range(3):
                a, c = block(i, j)
                parts.append(widened(k_ref[a, c, 64 * s : 64 * s + 64, :].astype(F32)))
            start = i * 256 + 64 * s if s < 4 else 768 + 64 * i
            dst_ref[start : start + 64, :] = pack3(*parts).astype(BF16)
    dst_ref[960:1024, :] = jnp.zeros((64, PK), BF16)


def fold(x):
    return jnp.sum(x.reshape(-1, 8, CP), axis=0)


def whole_sum(acc):
    return jnp.sum(acc, axis=0, keepdims=True)


def sigmoid(v):
    return 1.0 / (1.0 + jnp.exp(-v))


def sigmoid_by_tanh(v):
    return 0.5 + 0.5 * jnp.tanh(0.5 * v)


def kernel(
    f_hbm, k1_hbm, k2_hbm, u_hbm, g1_ref, s1_ref, g2_ref, s2_ref,
    out_hbm, g_hbm, pg_ref,
    fb, ub, gh, k1, k2, w1, b2, pad, x3, u3, y, gact, hid, a1t, a2t, gs,
    cbuf, s1buf, s2buf, s3buf, edge32, edge, rowbuf, colbuf, statbuf, pgbuf,
    in_sem, out_sem, hs_sem, hr_sem, ss_sem, sr_sem, ps_sem, pr_sem, rs_sem, rr_sem, free_sem,
):
    row, col, batch = lax.axis_index("row"), lax.axis_index("col"), lax.axis_index("batch")
    me = row * 2 + col
    core, near, deep = lax.rem(batch, 2), lax.rem(batch // 2, 2), batch // 4
    spot = (row, col * 2 + near, deep)
    inner = near * 2 + core

    def device(x=row, hi=col, lo=near, z=deep, side=core):
        return {"batch": (z * 2 + lo) * 2 + side, "row": x, "col": hi}

    def along(axis, d):
        j = lax.rem(spot[axis] + d, 4)
        if axis == 0:
            return j, device(x=j)
        if axis == 1:
            return j, device(hi=j // 2, lo=lax.rem(j, 2))
        return j, device(z=j)

    loads = [
        pltpu.make_async_copy(src, dst, in_sem.at[n])
        for n, (src, dst) in enumerate(((f_hbm.at[0], fb), (u_hbm.at[0], ub), (k1_hbm, k1), (k2_hbm, k2)))
    ]
    for copy in loads:
        copy.start()

    def peer(d):
        other = lax.rem(me + d, 8)
        return device(x=other // 2, hi=lax.rem(other, 2))

    barrier = pltpu.get_barrier_semaphore()
    others = [peer(d) for d in range(1, 8)] + [along(2, d)[1] for d in range(1, 4)]
    others += [device(side=1 - core), device(lo=1 - near), device(lo=1 - near, hi=1 - col)]
    others += [device(lo=1 - near, side=1 - core)]
    for other in others:
        pl.semaphore_signal(barrier, inc=1, device_id=other, device_id_type=MESH)
    pl.semaphore_wait(barrier, len(others))

    def stats_send(phase, first, second):
        statbuf[phase, me] = jnp.concatenate([first, second, jnp.zeros((6, CP), F32)], axis=0)
        copies = []
        for d in range(1, 8):
            copy = pltpu.make_async_remote_copy(
                statbuf.at[phase, me], statbuf.at[phase, me],
                ss_sem.at[phase, d - 1], sr_sem.at[phase, d - 1],
                device_id=peer(d), device_id_type=MESH,
            )
            copy.start()
            copies.append(copy)
        return copies

    def stats_get(phase, copies):
        for copy in copies:
            copy.wait()
        total = statbuf[phase, 0]
        for n in range(1, 8):
            total = total + statbuf[phase, n]
        return total

    def send(sems, index, src, dst, target):
        copy = pltpu.make_async_remote_copy(
            src, dst, sems[0].at[index], sems[1].at[index], device_id=target, device_id_type=MESH
        )
        copy.start()
        return copy

    def wait_all(copies):
        for copy in copies:
            copy.wait()

    mine = pl.ds(pl.multiple_of(core * 160, 8), 160)
    theirs = pl.ds(pl.multiple_of((1 - core) * 160, 8), 160)

    def forty(j):
        return pl.ds(pl.multiple_of(core * 160 + j * 40, 8), 40)

    def pair_send(k, a):
        t, cols = k // 2, pl.ds(k % 2 * 512, 512)
        return send(
            (rs_sem, rr_sem), (k, 0, a, 0), gs.at[t, a, theirs, cols], cbuf.at[k, a], device(side=1 - core)
        )

    def reduce_steps(k, pair):
        t, start = k // 2, k % 2 * 512
        wide = pl.ds(start, 512)

        def part(j):
            return pl.ds(pl.multiple_of(start + j * 128, 128), 128)

        axes = [[(a + n) % 3 for n in range(3)] for a in range(3)]
        rows = [forty(spot[axes[a][0]]) for a in range(3)]
        cols = [part(spot[axes[a][1]]) for a in range(3)]
        flying = [[], [], []]

        def sent(stage, a, targets):
            for target in targets:
                pl.semaphore_signal(free_sem.at[k, stage, a], inc=1, device_id=target, device_id_type=MESH)

        def ring(a, n):
            return [along(axes[a][n], d) for d in range(1, 4)]

        def targets(a, n):
            return [target for _, target in ring(a, n)]

        def fly(stage, a, src, dst, target, d=0):
            flying[a].append(send((rs_sem, rr_sem), (k, stage, a, d), src, dst, target))

        def landed(a):
            wait_all(flying[a])
            flying[a].clear()

        for a in range(3):
            pair[a].wait()
            sent(0, a, [device(side=1 - core)])
            gs[t, a, mine, wide] += cbuf[k, a]
            for d, (j, target) in enumerate(ring(a, 0)):
                fly(1, a, gs.at[t, a, forty(j), wide], s1buf.at[k, a, d], target, d)
        yield
        for a in range(3):
            landed(a)
            sent(1, a, targets(a, 0))
            gs[t, a, rows[a], wide] += s1buf[k, a, 0] + s1buf[k, a, 1] + s1buf[k, a, 2]
            for d, (j, target) in enumerate(ring(a, 1)):
                fly(2, a, gs.at[t, a, rows[a], part(j)], s2buf.at[k, a, d], target, d)
        yield
        for a in range(3):
            landed(a)
            sent(2, a, targets(a, 1))
            slot = spot[axes[a][2]]
            s3buf[k, a, slot] = gs[t, a, rows[a], cols[a]] + (s2buf[k, a, 0] + s2buf[k, a, 1] + s2buf[k, a, 2])
            for d, target in enumerate(targets(a, 2)):
                fly(3, a, s3buf.at[k, a, slot], s3buf.at[k, a, slot], target, d)
        yield
        for a in range(3):
            landed(a)
            gs[t, a, rows[a], cols[a]] = (s3buf[k, a, 0] + s3buf[k, a, 1]) + (s3buf[k, a, 2] + s3buf[k, a, 3])
            pl.semaphore_wait(free_sem.at[k, 2, a], 3)
            block = gs.at[t, a, rows[a], cols[a]]
            for d, target in enumerate(targets(a, 1)):
                fly(4, a, block, block, target, d)
        yield
        for a in range(3):
            landed(a)
            pl.semaphore_wait(free_sem.at[k, 1, a], 3)
            block = gs.at[t, a, rows[a], wide]
            for d, target in enumerate(targets(a, 0)):
                fly(5, a, block, block, target, d)
        yield
        for a in range(3):
            landed(a)
            pl.semaphore_wait(free_sem.at[k, 0, a], 1)
            block = gs.at[t, a, mine, wide]
            fly(6, a, block, block, device(side=1 - core))
        yield
        for a in range(3):
            landed(a)
        copy = pltpu.make_async_copy(gs.at[t, :, :, wide], g_hbm.at[t, :, :, wide], out_sem.at[k])
        copy.start()
        yield copy

    def param_steps(value):
        slots = (deep, inner)
        for n in range(2):
            slot = slots[n]
            pgbuf[n, slot] = value
            flying = []
            for d in range(1, 4):
                j = lax.rem(slot + d, 4)
                target = device(z=j) if n == 0 else device(lo=j // 2, side=lax.rem(j, 2))
                flying.append(send((ps_sem, pr_sem), (n, d - 1), pgbuf.at[n, slot], pgbuf.at[n, slot], target))
            yield
            wait_all(flying)
            value = (pgbuf[n, 0] + pgbuf[n, 1]) + (pgbuf[n, 2] + pgbuf[n, 3])
        pg_ref[...] = value
        yield

    gi = lax.broadcasted_iota(jnp.int32, (CP, CP), 0)
    gj = lax.broadcasted_iota(jnp.int32, (CP, CP), 1)
    same = ((gi * 6554) >> 16 == (gj * 6554) >> 16) & (gi < C) & (gj < C)
    member = jnp.where(same, 1.0, 0.0).astype(BF16)

    def group_means(rows):
        high = rows.astype(BF16)
        rest = rows - high.astype(F32)
        middle = rest.astype(BF16)
        low = (rest - middle.astype(F32)).astype(BF16)
        parts = [jnp.dot(v, member, preferred_element_type=F32) for v in (high, middle, low)]
        return (parts[0] + (parts[1] + parts[2])) / COUNT

    def norm_stats(total):
        means = group_means(total)
        mean = means[0:1]
        rstd = lax.rsqrt(means[1:2] - mean * mean + EPS)
        return mean, rstd

    up, down = lax.rem(row + 3, 4), lax.rem(row + 1, 4)
    across = 1 - col

    def halo_send(phase, src):
        edge[phase] = edge32[...].astype(BF16)
        moves = (
            (src.at[0], rowbuf.at[phase, 1], up, col),
            (src.at[R - 1], rowbuf.at[phase, 0], down, col),
            (edge.at[phase], colbuf.at[phase, 0], down, across),
            (edge.at[phase], colbuf.at[phase, 1], row, across),
            (edge.at[phase], colbuf.at[phase, 2], up, across),
        )
        copies = []
        for n, (a, b, r, c) in enumerate(moves):
            copy = pltpu.make_async_remote_copy(
                a, b, hs_sem.at[phase, n], hr_sem.at[phase, n],
                device_id=device(x=r, hi=c), device_id_type=MESH,
            )
            copy.start()
            copies.append(copy)
        return copies

    def take_edge(r, x):
        edge32[pl.ds(r, 1), :] = jnp.where(col == 0, x[W - 1 : W], x[0:1])

    def halo_fill(phase, fn):
        above, below = row > 0, row < 3
        for n, slot, ok in ((0, 0, above), (1, R + 1, below)):
            v = fn(widened(rowbuf[phase, n].astype(F32)))
            pad[slot, 8 : 8 + W, :] = jnp.where(ok, v, 0.0)
        v0 = jnp.where(above, fn(colbuf[phase, 0].astype(F32)), 0.0)
        v1 = fn(colbuf[phase, 1].astype(F32))
        v2 = jnp.where(below, fn(colbuf[phase, 2].astype(F32)), 0.0)
        for slot in range(R + 2):
            line = v0[R - 1 : R] if slot == 0 else v2[0:1] if slot == R + 1 else v1[slot - 1 : slot]
            pad[slot, 7:8, :] = jnp.where(col == 1, line, 0.0)
            pad[slot, 8 + W : 9 + W, :] = jnp.where(col == 0, line, 0.0)

    def build(dst):
        @pl.loop(0, R + 2)
        def _(s):
            x = pad[s, 8 : 8 + W, :]
            place = lax.broadcasted_iota(jnp.int32, x.shape, 0)
            before = jnp.where(place == 0, pad[s, 7:8, :], pltpu.roll(x, 1, 0))
            after = jnp.where(place == W - 1, pad[s, 8 + W : 9 + W, :], pltpu.roll(x, W - 1, 0))
            dst[pl.ds(pl.multiple_of(s * W, W), W), :] = pack3(before, x, after).astype(BF16)

    def conv(src, weights, transposed, first=0, last=3):
        dims = (((1,), (1 if transposed else 0,)), ((), ()))

        @pl.loop(first, last)
        def _(s):
            rows = pl.ds(pl.multiple_of(s * 768, 768), 768)
            y[rows, :] = lax.dot_general(src[rows, :], weights[...], dims, preferred_element_type=F32)

    def combined(p, size):
        r0 = pl.ds(p, size)
        r1 = pl.ds(p + W, size)
        r2 = pl.ds(p + 2 * W, size)
        main = y[r0, 0:256] + y[r1, 256:512] + y[r2, 512:768]
        tail = y[r0, 768:896] + pltpu.roll(y[r1, 768:896], 64, 1) + y[r2, 896:1024]
        low = lax.broadcasted_iota(jnp.int32, tail.shape, 1) < 64
        return jnp.concatenate([main, jnp.where(low, tail, 0.0)], axis=1)

    def chunks(body, init):
        def step(n, carry):
            return body(pl.multiple_of(n * CHUNK, CHUNK), carry)

        return lax.fori_loop(0, PX // CHUNK, step, init)

    def kernel_grad(left, right, k, between=lambda a: None):
        t, cols = k // 2, slice(k % 2 * 512, k % 2 * 512 + 512)
        pair = []
        for a in range(3):
            rows = slice((2 - a) * W, (2 - a) * W + PX)
            gs[t, a, :, cols] = jnp.dot(left[...], right[rows, cols], preferred_element_type=F32)
            pair.append(pair_send(k, a))
            between(a)
        return reduce_steps(k, pair)

    zero = jnp.zeros((8, CP), F32)
    g1, s1, g2, s2 = (widened(v[...].reshape(1, C)) for v in (g1_ref, s1_ref, g2_ref, s2_ref))

    loads[0].wait()

    def first_stats(r, carry):
        total, square = carry
        x = widened(fb[r].astype(F32))
        take_edge(r, x)
        return total + fold(x), square + fold(x * x)

    total, square = lax.fori_loop(0, R, first_stats, (zero, zero))
    sent_one = stats_send(0, whole_sum(total), whole_sum(square))
    halo_one = halo_send(0, fb)

    loads[1].wait()

    @pl.loop(0, R)
    def _(r):
        x = widened(ub[r].astype(F32))
        take_edge(r, x)
        pad[r + 1, 8 : 8 + W, :] = x

    halo_up = halo_send(1, ub)
    loads[2].wait()
    pack_weights(k1, w1, lambda i, j: (j, i))
    loads[3].wait()
    pack_weights(k2, b2, lambda i, j: (2 - i, 2 - j))
    for copy in halo_up:
        copy.wait()
    halo_fill(1, lambda v: v)
    build(u3)

    mean1, rstd1 = norm_stats(stats_get(0, sent_one))
    scale1 = rstd1 * g1
    for copy in halo_one:
        copy.wait()

    def act_one(x):
        v = (x - mean1) * scale1 + s1
        return (v * sigmoid_by_tanh(v)).astype(BF16).astype(F32)

    @pl.loop(0, R * 4)
    def _(n):
        r, q = n // 4, lax.rem(n, 4)
        p = pl.multiple_of(q * CHUNK, CHUNK)
        pad[r + 1, pl.ds(8 + p, CHUNK), :] = act_one(widened(fb[r, pl.ds(p, CHUNK), :].astype(F32)))

    halo_fill(0, act_one)
    build(x3)
    conv(x3, w1, False)

    def hidden_stats(p, carry):
        total, square = carry
        h = combined(p, CHUNK).astype(BF16)
        hid[pl.ds(p, CHUNK), :] = h
        h = h.astype(F32)
        return total + fold(h), square + fold(h * h)

    total, square = chunks(hidden_stats, (zero, zero))
    sent_two = stats_send(1, whole_sum(total), whole_sum(square))

    conv(u3, b2, True)

    @pl.loop(0, R)
    def _(r):
        where = pl.ds(pl.multiple_of(r * W, W), W)
        a1t[:, where] = pad[r + 1, 8 : 8 + W, :].T[:C].astype(BF16)

    mean2, rstd2 = norm_stats(stats_get(1, sent_two))
    scale2 = rstd2 * g2

    def second_back(p, carry):
        shift, gain = carry
        here = pl.ds(p, CHUNK)
        q = pl.multiple_of(8 + lax.rem(p, W), 8)
        centred = hid[here, :].astype(F32) - mean2
        pre = centred * scale2 + s2
        s = sigmoid(pre)
        pad[p // W + 1, pl.ds(q, CHUNK), :] = pre * s
        gp = combined(p, CHUNK) * s * (1.0 + pre * (1.0 - s))
        gact[here, :] = gp
        return shift + fold(gp), gain + fold(gp * centred)

    shift, gain = chunks(second_back, (zero, zero))
    shift2, gain2 = whole_sum(shift), whole_sum(gain) * rstd2
    sent_three = stats_send(2, shift2, gain2)

    @pl.loop(0, R)
    def _(r):
        where = pl.ds(pl.multiple_of(r * W, W), W)
        a2t[:, where] = pad[r + 1, 8 : 8 + W, :].T[:C].astype(BF16)

    sum_a = kernel_grad(a2t, u3, 0)
    total2 = stats_get(2, sent_three)
    means = group_means(total2 * g2)
    m1, m2 = means[0:1] * rstd2, means[1:2] * (rstd2 * rstd2)

    @pl.loop(0, R)
    def _(r):
        for q in range(W // CHUNK):
            here = pl.ds(pl.multiple_of(r * W + q * CHUNK, CHUNK), CHUNK)
            centred = hid[here, :].astype(F32) - mean2
            v = (gact[here, :] * scale2 - m1 - centred * m2).astype(BF16)
            gh[r, q * CHUNK : q * CHUNK + CHUNK, :] = v[:, :C]
            pad[r + 1, 8 + q * CHUNK : 8 + q * CHUNK + CHUNK, :] = v.astype(F32)
        edge32[pl.ds(r, 1), :] = jnp.where(
            col == 0, pad[r + 1, 7 + W : 8 + W, :], pad[r + 1, 8:9, :]
        )

    halo_gh = halo_send(2, gh)
    next(sum_a)
    sum_b = kernel_grad(a2t, u3, 1)
    pack_weights(k1, w1, lambda i, j: (2 - i, 2 - j))
    for copy in halo_gh:
        copy.wait()
    halo_fill(2, lambda v: v)
    next(sum_a)
    next(sum_b)
    build(x3)
    next(sum_a)
    sum_c = kernel_grad(a1t, x3, 2, lambda a: next(sum_b) if a == 1 else next(sum_a) if a == 2 else None)
    sum_d = kernel_grad(a1t, x3, 3, lambda a: next(sum_b) if a == 0 else None)
    next(sum_c)
    next(sum_b)
    conv(x3, w1, True, 0, 1)
    next(sum_d)
    conv(x3, w1, True, 1, 3)
    next(sum_c)
    next(sum_a)

    def centred_one(r, p):
        return widened(fb[r, pl.ds(p, CHUNK), :].astype(F32)) - mean1

    def first_back(n, carry):
        shift, gain = carry
        r, q = n // 4, lax.rem(n, 4)
        p = pl.multiple_of(n * CHUNK, CHUNK)
        centred = centred_one(r, pl.multiple_of(q * CHUNK, CHUNK))
        pre = centred * scale1 + s1
        s = sigmoid_by_tanh(pre)
        gp = combined(p, CHUNK) * s * (1.0 + pre * (1.0 - s))
        gact[pl.ds(p, CHUNK), :] = gp
        return shift + fold(gp), gain + fold(gp * centred)

    carry = (zero, zero)
    for part, steps in enumerate(((sum_d,), (sum_c, sum_b), (sum_d,), (sum_c,))):
        carry = lax.fori_loop(part * 16, part * 16 + 16, first_back, carry)
        for step in steps:
            next(step)
    shift, gain = carry
    shift1, gain1 = whole_sum(shift), whole_sum(gain) * rstd1
    sent_four = stats_send(3, shift1, gain1)
    next(sum_a)
    total1 = stats_get(3, sent_four)
    next(sum_d)
    means = group_means(total1 * g1)
    steps_p = param_steps(
        jnp.concatenate([total1[1:2], total1[0:1], total2[1:2], total2[0:1], jnp.zeros((4, CP), F32)], axis=0)
    )
    next(steps_p)
    n_one, n_two = means[0:1] * rstd1, means[1:2] * (rstd1 * rstd1)

    def finish(n):
        r, q = n // 4, lax.rem(n, 4)
        p = pl.multiple_of(q * CHUNK, CHUNK)
        here = pl.ds(pl.multiple_of(n * CHUNK, CHUNK), CHUNK)
        v = gact[here, :] * scale1 - n_one - centred_one(r, p) * n_two
        gh[r, pl.ds(p, CHUNK), :] = (ub[r, pl.ds(p, CHUNK), :].astype(F32) + v[:, :C]).astype(BF16)

    pl.loop(0, 32)(finish)
    next(sum_c)
    next(sum_b)
    pl.loop(32, 64)(finish)
    outs = [pltpu.make_async_copy(gh, out_hbm.at[0], out_sem.at[4])]
    outs[0].start()
    next(sum_d)
    outs.append(next(sum_a))
    next(steps_p)
    outs.append(next(sum_b))
    next(sum_c)
    next(steps_p)
    next(sum_d)
    outs.append(next(sum_c))
    outs.append(next(sum_d))
    for copy in outs:
        copy.wait()


def unpack(g_ref, g1_ref, g2_ref):
    for t, dst in ((0, g2_ref), (1, g1_ref)):
        for c in range(3):
            b = 2 - c
            dst[0, c, :, 0:256] = g_ref[t, 0, :, b * 256 : b * 256 + 256]
            x = g_ref[t, 0, :, 896:1024] if b == 2 else g_ref[t, 0, :, 768:896]
            if b == 1:
                x = pltpu.roll(x, 64, 1)
            dst[0, c, :, 256:320] = x[:, 0:64]


def per_device(features, first_kernel, second_kernel, first_gain, first_shift, second_gain, second_shift, upstream):
    params = [first_gain, first_shift, second_gain, second_shift]
    hbm = pl.BlockSpec(memory_space=pl.ANY)
    vmem = pl.BlockSpec(memory_space=pltpu.VMEM)
    input_grad, packed, pg = pl.pallas_call(
        kernel,
        out_shape=(
            jax.ShapeDtypeStruct((1, R, W, C), BF16),
            jax.ShapeDtypeStruct((2, 3, C, PK), F32),
            jax.ShapeDtypeStruct((8, CP), F32),
        ),
        in_specs=[hbm, hbm, hbm, hbm, vmem, vmem, vmem, vmem],
        out_specs=(hbm, hbm, vmem),
        scratch_shapes=[
            pltpu.VMEM((R, W, C), BF16),
            pltpu.VMEM((R, W, C), BF16),
            pltpu.VMEM((R, W, C), BF16),
            pltpu.VMEM((3, 3, C, C), BF16),
            pltpu.VMEM((3, 3, C, C), BF16),
            pltpu.VMEM((PK, PK), BF16),
            pltpu.VMEM((PK, PK), BF16),
            pltpu.VMEM((R + 2, W + 16, CP), F32),
            pltpu.VMEM(((R + 2) * W, PK), BF16),
            pltpu.VMEM(((R + 2) * W, PK), BF16),
            pltpu.VMEM(((R + 2) * W, PK), F32),
            pltpu.VMEM((PX, CP), F32),
            pltpu.VMEM((PX, CP), BF16),
            pltpu.VMEM((C, PX), BF16),
            pltpu.VMEM((C, PX), BF16),
            pltpu.VMEM((2, 3, C, PK), F32),
            pltpu.VMEM((4, 3, 160, 512), F32),
            pltpu.VMEM((4, 3, 3, 40, 512), F32),
            pltpu.VMEM((4, 3, 3, 40, 128), F32),
            pltpu.VMEM((4, 3, 4, 40, 128), F32),
            pltpu.VMEM((R, CP), F32),
            pltpu.VMEM((3, R, CP), BF16),
            pltpu.VMEM((3, 2, W, C), BF16),
            pltpu.VMEM((3, 3, R, CP), BF16),
            pltpu.VMEM((4, 8, 8, CP), F32),
            pltpu.VMEM((2, 4, 8, CP), F32),
            pltpu.SemaphoreType.DMA((4,)),
            pltpu.SemaphoreType.DMA((5,)),
            pltpu.SemaphoreType.DMA((3, 5)),
            pltpu.SemaphoreType.DMA((3, 5)),
            pltpu.SemaphoreType.DMA((4, 7)),
            pltpu.SemaphoreType.DMA((4, 7)),
            pltpu.SemaphoreType.DMA((2, 3)),
            pltpu.SemaphoreType.DMA((2, 3)),
            pltpu.SemaphoreType.DMA((4, 7, 3, 3)),
            pltpu.SemaphoreType.DMA((4, 7, 3, 3)),
            pltpu.SemaphoreType.REGULAR((4, 3, 3)),
        ],
        compiler_params=pltpu.CompilerParams(
            collective_id=0, has_side_effects=True, vmem_limit_bytes=67_000_000
        ),
        name="resblock_backward",
    )(features, first_kernel, second_kernel, upstream, *params)
    grad = jax.ShapeDtypeStruct((3, 3, C, C), F32)
    taps = pl.BlockSpec((1, 3, C, C), lambda a: (a, 0, 0, 0))
    g1, g2 = pl.pallas_call(
        unpack,
        grid=(3,),
        out_shape=(grad, grad),
        in_specs=[pl.BlockSpec((2, 1, C, PK), lambda a: (0, a, 0, 0))],
        out_specs=(taps, taps),
        name="unpack",
    )(packed)
    return input_grad, g1, g2, pg[:4, :C]


def solution(mesh):
    tiles = P("batch", "row", "col", None)
    return jax.shard_map(
        per_device,
        mesh=mesh,
        in_specs=(tiles, P(), P(), P(), P(), P(), P(), tiles),
        out_specs=(tiles, P(), P(), P()),
        check_vma=False,
    )
```

```python
import jax
import jax.numpy as jnp
from jax import lax
from jax.experimental import pallas as pl
from jax.experimental.pallas import tpu as pltpu
from jax.sharding import PartitionSpec as P

GROUPS = 32
EPS = 1e-05
R, W, C, CP = 16, 128, 320, 384
PX = R * W
PK = 1024
CHUNK = 32
COUNT = float(64 * 256 * (C // GROUPS))
F32, BF16 = jnp.float32, jnp.bfloat16
MESH = pl.DeviceIdType.MESH


def widened(v):
    return jnp.concatenate([v, jnp.zeros((v.shape[0], CP - C), v.dtype)], axis=1)


def pack3(x0, x1, x2):
    t0, t1, t2 = (x[:, 256:384] for x in (x0, x1, x2))
    low = lax.broadcasted_iota(jnp.int32, t0.shape, 1) < 64
    mid = jnp.where(low, t0, pltpu.roll(t1, 64, 1))
    end = jnp.where(low, t2, 0.0)
    return jnp.concatenate([x0[:, :256], x1[:, :256], x2[:, :256], mid, end], axis=1)


def pack_weights(k_ref, dst_ref, block):
    for i in range(3):
        for s in range(5):
            parts = []
            for j in range(3):
                a, c = block(i, j)
                parts.append(widened(k_ref[a, c, 64 * s : 64 * s + 64, :].astype(F32)))
            start = i * 256 + 64 * s if s < 4 else 768 + 64 * i
            dst_ref[start : start + 64, :] = pack3(*parts).astype(BF16)
    dst_ref[960:1024, :] = jnp.zeros((64, PK), BF16)


def fold(x):
    return jnp.sum(x.reshape(-1, 8, CP), axis=0)


def whole_sum(acc):
    return jnp.sum(acc, axis=0, keepdims=True)


def sigmoid(v):
    return 1.0 / (1.0 + jnp.exp(-v))


def sigmoid_by_tanh(v):
    return 0.5 + 0.5 * jnp.tanh(0.5 * v)


def kernel(
    f_hbm, k1_hbm, k2_hbm, u_hbm, g1_ref, s1_ref, g2_ref, s2_ref,
    out_hbm, g_hbm, pg_ref,
    fb, ub, gh, k1, k2, w1, b2, pad, x3, u3, y, gact, hid, a1t, a2t, gs,
    c0buf, s10buf, s20buf, s30buf, c1buf, s11buf, s21buf, s31buf, edge32, edge, rowbuf, colbuf, statbuf, pgbuf,
    in_sem, out_sem, hs_sem, hr_sem, ss_sem, sr_sem, ps_sem, pr_sem, rs_sem, rr_sem, free_sem,
):
    row, col, batch = lax.axis_index("row"), lax.axis_index("col"), lax.axis_index("batch")
    me = row * 2 + col
    core, near, deep = lax.rem(batch, 2), lax.rem(batch // 2, 2), batch // 4
    spot = (row, col * 2 + near, deep)
    inner = near * 2 + core

    def device(x=row, hi=col, lo=near, z=deep, side=core):
        return {"batch": (z * 2 + lo) * 2 + side, "row": x, "col": hi}

    def along(axis, d):
        j = lax.rem(spot[axis] + d, 4)
        if axis == 0:
            return j, device(x=j)
        if axis == 1:
            return j, device(hi=j // 2, lo=lax.rem(j, 2))
        return j, device(z=j)

    def slot(r):
        return pl.ds(pl.multiple_of(lax.rem(r, 7) * C, 16), C), pl.ds(pl.multiple_of(r // 7 * 128, 128), 128)

    loads = [[], [], [], []]
    for n, (src, dst) in enumerate(((f_hbm, x3), (u_hbm, u3))):
        for r in range(R):
            rows, cols = slice(r % 7 * C, r % 7 * C + C), slice(r // 7 * 128, r // 7 * 128 + 128)
            loads[n].append(pltpu.make_async_copy(src.at[0, r], dst.at[rows, cols], in_sem.at[n, r]))
    for n, (src, dst) in enumerate(((k1_hbm, k1), (k2_hbm, k2))):
        loads[2 + n].append(pltpu.make_async_copy(src, dst, in_sem.at[2, n]))
    for group in loads:
        for copy in group:
            copy.start()

    def turned(ref, r):
        rows, cols = slot(r)
        v = ref[rows, cols].astype(F32)
        return jnp.concatenate([v, jnp.zeros((CP - C, W), F32)], axis=0).T

    def peer(d):
        other = lax.rem(me + d, 8)
        return device(x=other // 2, hi=lax.rem(other, 2))

    barrier = pltpu.get_barrier_semaphore()
    others = [peer(d) for d in range(1, 8)] + [along(2, d)[1] for d in range(1, 4)]
    others += [device(side=1 - core), device(lo=1 - near), device(lo=1 - near, hi=1 - col)]
    others += [device(lo=1 - near, side=1 - core)]
    for other in others:
        pl.semaphore_signal(barrier, inc=1, device_id=other, device_id_type=MESH)
    pl.semaphore_wait(barrier, len(others))

    def stats_send(phase, first, second):
        statbuf[phase, me] = jnp.concatenate([first, second, jnp.zeros((6, CP), F32)], axis=0)
        copies = []
        for d in range(1, 8):
            copy = pltpu.make_async_remote_copy(
                statbuf.at[phase, me], statbuf.at[phase, me],
                ss_sem.at[phase, d - 1], sr_sem.at[phase, d - 1],
                device_id=peer(d), device_id_type=MESH,
            )
            copy.start()
            copies.append(copy)
        return copies

    def stats_get(phase, copies):
        for copy in copies:
            copy.wait()
        total = statbuf[phase, 0]
        for n in range(1, 8):
            total = total + statbuf[phase, n]
        return total

    def send(sems, index, src, dst, target):
        copy = pltpu.make_async_remote_copy(
            src, dst, sems[0].at[index], sems[1].at[index], device_id=target, device_id_type=MESH
        )
        copy.start()
        return copy

    def wait_all(copies):
        for copy in copies:
            copy.wait()

    mine = pl.ds(pl.multiple_of(core * 160, 8), 160)
    theirs = pl.ds(pl.multiple_of((1 - core) * 160, 8), 160)

    def forty(j):
        return pl.ds(pl.multiple_of(core * 160 + j * 40, 8), 40)

    whole = (c0buf, s10buf, s20buf, s30buf)
    halves = [[ref.at[n] for ref in (c1buf, s11buf, s21buf, s31buf)] for n in range(2)]
    chains = ((0, 0, PK, whole), (1, 0, 512, halves[0]), (1, 512, 512, halves[1]))

    def pair_send(k, a):
        t, start, width, (cbuf, _, _, _) = chains[k]
        return send(
            (rs_sem, rr_sem), (k, 0, a, 0), gs.at[t, a, theirs, pl.ds(start, width)], cbuf.at[a],
            device(side=1 - core),
        )

    def reduce_steps(k, pair):
        t, start, width, (cbuf, s1buf, s2buf, s3buf) = chains[k]
        wide = pl.ds(start, width)

        def part(j):
            return pl.ds(pl.multiple_of(start + j * (width // 4), 128), width // 4)

        axes = [[(a + n) % 3 for n in range(3)] for a in range(3)]
        rows = [forty(spot[axes[a][0]]) for a in range(3)]
        cols = [part(spot[axes[a][1]]) for a in range(3)]
        flying = [[], [], []]

        def sent(stage, a, targets):
            for target in targets:
                pl.semaphore_signal(free_sem.at[k, stage, a], inc=1, device_id=target, device_id_type=MESH)

        def ring(a, n):
            return [along(axes[a][n], d) for d in range(1, 4)]

        def targets(a, n):
            return [target for _, target in ring(a, n)]

        def fly(stage, a, src, dst, target, d=0):
            flying[a].append(send((rs_sem, rr_sem), (k, stage, a, d), src, dst, target))

        def landed(a):
            wait_all(flying[a])
            flying[a].clear()

        for a in range(3):
            pair[a].wait()
            sent(0, a, [device(side=1 - core)])
            gs[t, a, mine, wide] += cbuf[a]
            for d, (j, target) in enumerate(ring(a, 0)):
                fly(1, a, gs.at[t, a, forty(j), wide], s1buf.at[a, d], target, d)
        yield
        for a in range(3):
            landed(a)
            sent(1, a, targets(a, 0))
            gs[t, a, rows[a], wide] += s1buf[a, 0] + s1buf[a, 1] + s1buf[a, 2]
            for d, (j, target) in enumerate(ring(a, 1)):
                fly(2, a, gs.at[t, a, rows[a], part(j)], s2buf.at[a, d], target, d)
        yield
        for a in range(3):
            landed(a)
            sent(2, a, targets(a, 1))
            slot = spot[axes[a][2]]
            s3buf[a, slot] = gs[t, a, rows[a], cols[a]] + (s2buf[a, 0] + s2buf[a, 1] + s2buf[a, 2])
            for d, target in enumerate(targets(a, 2)):
                fly(3, a, s3buf.at[a, slot], s3buf.at[a, slot], target, d)
        yield
        for a in range(3):
            landed(a)
            gs[t, a, rows[a], cols[a]] = (s3buf[a, 0] + s3buf[a, 1]) + (s3buf[a, 2] + s3buf[a, 3])
            pl.semaphore_wait(free_sem.at[k, 2, a], 3)
            block = gs.at[t, a, rows[a], cols[a]]
            for d, target in enumerate(targets(a, 1)):
                fly(4, a, block, block, target, d)
        yield
        for a in range(3):
            landed(a)
            pl.semaphore_wait(free_sem.at[k, 1, a], 3)
            block = gs.at[t, a, rows[a], wide]
            for d, target in enumerate(targets(a, 0)):
                fly(5, a, block, block, target, d)
        yield
        for a in range(3):
            landed(a)
            pl.semaphore_wait(free_sem.at[k, 0, a], 1)
            block = gs.at[t, a, mine, wide]
            fly(6, a, block, block, device(side=1 - core))
        yield
        for a in range(3):
            landed(a)
        copy = pltpu.make_async_copy(gs.at[t, :, :, wide], g_hbm.at[t, :, :, wide], out_sem.at[k])
        copy.start()
        yield copy

    def param_steps(value):
        slots = (deep, inner)
        for n in range(2):
            slot = slots[n]
            pgbuf[n, slot] = value
            flying = []
            for d in range(1, 4):
                j = lax.rem(slot + d, 4)
                target = device(z=j) if n == 0 else device(lo=j // 2, side=lax.rem(j, 2))
                flying.append(send((ps_sem, pr_sem), (n, d - 1), pgbuf.at[n, slot], pgbuf.at[n, slot], target))
            yield
            wait_all(flying)
            value = (pgbuf[n, 0] + pgbuf[n, 1]) + (pgbuf[n, 2] + pgbuf[n, 3])
        pg_ref[...] = value
        yield

    gi = lax.broadcasted_iota(jnp.int32, (CP, CP), 0)
    gj = lax.broadcasted_iota(jnp.int32, (CP, CP), 1)
    same = ((gi * 6554) >> 16 == (gj * 6554) >> 16) & (gi < C) & (gj < C)
    member = jnp.where(same, 1.0, 0.0).astype(BF16)

    def group_means(rows):
        high = rows.astype(BF16)
        rest = rows - high.astype(F32)
        middle = rest.astype(BF16)
        low = (rest - middle.astype(F32)).astype(BF16)
        parts = [jnp.dot(v, member, preferred_element_type=F32) for v in (high, middle, low)]
        return (parts[0] + (parts[1] + parts[2])) / COUNT

    def norm_stats(total):
        means = group_means(total)
        mean = means[0:1]
        rstd = lax.rsqrt(means[1:2] - mean * mean + EPS)
        return mean, rstd

    up, down = lax.rem(row + 3, 4), lax.rem(row + 1, 4)
    across = 1 - col

    def halo_send(phase, src):
        edge[phase] = edge32[...].astype(BF16)
        moves = (
            (src.at[0], rowbuf.at[phase, 1], up, col),
            (src.at[R - 1], rowbuf.at[phase, 0], down, col),
            (edge.at[phase], colbuf.at[phase, 0], down, across),
            (edge.at[phase], colbuf.at[phase, 1], row, across),
            (edge.at[phase], colbuf.at[phase, 2], up, across),
        )
        copies = []
        for n, (a, b, r, c) in enumerate(moves):
            copy = pltpu.make_async_remote_copy(
                a, b, hs_sem.at[phase, n], hr_sem.at[phase, n],
                device_id=device(x=r, hi=c), device_id_type=MESH,
            )
            copy.start()
            copies.append(copy)
        return copies

    def take_edge(r, x):
        edge32[pl.ds(r, 1), :] = jnp.where(col == 0, x[W - 1 : W], x[0:1])

    def halo_fill(phase, fn):
        above, below = row > 0, row < 3
        for n, slot, ok in ((0, 0, above), (1, R + 1, below)):
            v = fn(widened(rowbuf[phase, n].astype(F32)))
            pad[slot, 8 : 8 + W, :] = jnp.where(ok, v, 0.0)
        v0 = jnp.where(above, fn(colbuf[phase, 0].astype(F32)), 0.0)
        v1 = fn(colbuf[phase, 1].astype(F32))
        v2 = jnp.where(below, fn(colbuf[phase, 2].astype(F32)), 0.0)
        for slot in range(R + 2):
            line = v0[R - 1 : R] if slot == 0 else v2[0:1] if slot == R + 1 else v1[slot - 1 : slot]
            pad[slot, 7:8, :] = jnp.where(col == 1, line, 0.0)
            pad[slot, 8 + W : 9 + W, :] = jnp.where(col == 0, line, 0.0)

    def build(dst):
        @pl.loop(0, R + 2)
        def _(s):
            x = pad[s, 8 : 8 + W, :]
            place = lax.broadcasted_iota(jnp.int32, x.shape, 0)
            before = jnp.where(place == 0, pad[s, 7:8, :], pltpu.roll(x, 1, 0))
            after = jnp.where(place == W - 1, pad[s, 8 + W : 9 + W, :], pltpu.roll(x, W - 1, 0))
            dst[pl.ds(pl.multiple_of(s * W, W), W), :] = pack3(before, x, after).astype(BF16)

    def conv(src, weights, transposed, first=0, last=3):
        dims = (((1,), (1 if transposed else 0,)), ((), ()))

        @pl.loop(first, last)
        def _(s):
            rows = pl.ds(pl.multiple_of(s * 768, 768), 768)
            y[rows, :] = lax.dot_general(src[rows, :], weights[...], dims, preferred_element_type=F32)

    def combined(p, size):
        r0 = pl.ds(p, size)
        r1 = pl.ds(p + W, size)
        r2 = pl.ds(p + 2 * W, size)
        main = y[r0, 0:256] + y[r1, 256:512] + y[r2, 512:768]
        tail = y[r0, 768:896] + pltpu.roll(y[r1, 768:896], 64, 1) + y[r2, 896:1024]
        low = lax.broadcasted_iota(jnp.int32, tail.shape, 1) < 64
        return jnp.concatenate([main, jnp.where(low, tail, 0.0)], axis=1)

    def chunks(body, init):
        def step(n, carry):
            return body(pl.multiple_of(n * CHUNK, CHUNK), carry)

        return lax.fori_loop(0, PX // CHUNK, step, init)

    def kernel_dot(left, right, t, start, a):
        rows, cols = slice((2 - a) * W, (2 - a) * W + PX), slice(start, start + 512)
        gs[t, a, :, cols] = jnp.dot(left[...], right[rows, cols], preferred_element_type=F32)

    def kernel_grad(left, right, k):
        pair = []
        for a in range(3):
            kernel_dot(left, right, chains[k][0], chains[k][1], a)
            pair.append(pair_send(k, a))
        return reduce_steps(k, pair)

    zero = jnp.zeros((8, CP), F32)
    g1, s1, g2, s2 = (widened(v[...].reshape(1, C)) for v in (g1_ref, s1_ref, g2_ref, s2_ref))

    wait_all(loads[0])

    def first_stats(r, carry):
        total, square = carry
        x = turned(x3, r)
        fb[r] = x[:, :C].astype(BF16)
        take_edge(r, x)
        return total + fold(x), square + fold(x * x)

    total, square = lax.fori_loop(0, R, first_stats, (zero, zero))
    sent_one = stats_send(0, whole_sum(total), whole_sum(square))
    halo_one = halo_send(0, fb)

    wait_all(loads[1])

    @pl.loop(0, R)
    def _(r):
        x = turned(u3, r)
        ub[r] = x[:, :C].astype(BF16)
        take_edge(r, x)

    halo_up = halo_send(1, ub)
    wait_all(loads[2])
    pack_weights(k1, w1, lambda i, j: (j, i))
    wait_all(loads[3])
    pack_weights(k2, b2, lambda i, j: (2 - i, 2 - j))

    mean1, rstd1 = norm_stats(stats_get(0, sent_one))
    scale1 = rstd1 * g1
    for copy in halo_one:
        copy.wait()

    def act_one(x):
        v = (x - mean1) * scale1 + s1
        return (v * sigmoid_by_tanh(v)).astype(BF16).astype(F32)

    @pl.loop(0, R * 4)
    def _(n):
        r, q = n // 4, lax.rem(n, 4)
        p = pl.multiple_of(q * CHUNK, CHUNK)
        pad[r + 1, pl.ds(8 + p, CHUNK), :] = act_one(widened(fb[r, pl.ds(p, CHUNK), :].astype(F32)))

    halo_fill(0, act_one)
    build(x3)
    conv(x3, w1, False)

    def hidden_stats(p, carry):
        total, square = carry
        h = combined(p, CHUNK).astype(BF16)
        hid[pl.ds(p, CHUNK), :] = h
        h = h.astype(F32)
        return total + fold(h), square + fold(h * h)

    total, square = chunks(hidden_stats, (zero, zero))
    sent_two = stats_send(1, whole_sum(total), whole_sum(square))

    @pl.loop(0, R)
    def _(r):
        where = pl.ds(pl.multiple_of(r * W, W), W)
        a1t[:, where] = pad[r + 1, 8 : 8 + W, :].T[:C].astype(BF16)
        pad[r + 1, 8 : 8 + W, :] = widened(ub[r].astype(F32))

    wait_all(halo_up)
    halo_fill(1, lambda v: v)
    build(u3)
    conv(u3, b2, True)

    mean2, rstd2 = norm_stats(stats_get(1, sent_two))
    scale2 = rstd2 * g2

    def second_back(p, carry):
        shift, gain = carry
        here = pl.ds(p, CHUNK)
        q = pl.multiple_of(8 + lax.rem(p, W), 8)
        centred = hid[here, :].astype(F32) - mean2
        pre = centred * scale2 + s2
        s = sigmoid(pre)
        pad[p // W + 1, pl.ds(q, CHUNK), :] = pre * s
        gp = combined(p, CHUNK) * s * (1.0 + pre * (1.0 - s))
        gact[here, :] = gp
        return shift + fold(gp), gain + fold(gp * centred)

    shift, gain = chunks(second_back, (zero, zero))
    shift2, gain2 = whole_sum(shift), whole_sum(gain) * rstd2
    sent_three = stats_send(2, shift2, gain2)

    @pl.loop(0, R)
    def _(r):
        where = pl.ds(pl.multiple_of(r * W, W), W)
        a2t[:, where] = pad[r + 1, 8 : 8 + W, :].T[:C].astype(BF16)

    for a in range(3):
        kernel_dot(a2t, u3, 0, 0, a)
    total2 = stats_get(2, sent_three)
    means = group_means(total2 * g2)
    m1, m2 = means[0:1] * rstd2, means[1:2] * (rstd2 * rstd2)

    @pl.loop(0, R)
    def _(r):
        for q in range(W // CHUNK):
            here = pl.ds(pl.multiple_of(r * W + q * CHUNK, CHUNK), CHUNK)
            centred = hid[here, :].astype(F32) - mean2
            v = (gact[here, :] * scale2 - m1 - centred * m2).astype(BF16)
            gh[r, q * CHUNK : q * CHUNK + CHUNK, :] = v[:, :C]
            pad[r + 1, 8 + q * CHUNK : 8 + q * CHUNK + CHUNK, :] = v.astype(F32)
        edge32[pl.ds(r, 1), :] = jnp.where(
            col == 0, pad[r + 1, 7 + W : 8 + W, :], pad[r + 1, 8:9, :]
        )

    halo_gh = halo_send(2, gh)
    pair = []
    for a in range(3):
        kernel_dot(a2t, u3, 0, 512, a)
        pair.append(pair_send(0, a))
    sum_a = reduce_steps(0, pair)
    pack_weights(k1, w1, lambda i, j: (2 - i, 2 - j))
    wait_all(halo_gh)
    next(sum_a)
    halo_fill(2, lambda v: v)
    build(x3)
    sum_c = kernel_grad(a1t, x3, 1)
    sum_d = kernel_grad(a1t, x3, 2)
    next(sum_c)
    next(sum_a)
    conv(x3, w1, True, 0, 1)
    next(sum_d)
    next(sum_a)
    conv(x3, w1, True, 1, 3)
    next(sum_c)
    next(sum_a)

    def centred_one(r, p):
        return widened(fb[r, pl.ds(p, CHUNK), :].astype(F32)) - mean1

    def first_back(n, carry):
        shift, gain = carry
        r, q = n // 4, lax.rem(n, 4)
        p = pl.multiple_of(n * CHUNK, CHUNK)
        centred = centred_one(r, pl.multiple_of(q * CHUNK, CHUNK))
        pre = centred * scale1 + s1
        s = sigmoid_by_tanh(pre)
        gp = combined(p, CHUNK) * s * (1.0 + pre * (1.0 - s))
        gact[pl.ds(p, CHUNK), :] = gp
        return shift + fold(gp), gain + fold(gp * centred)

    carry = (zero, zero)
    for part, steps in enumerate(((sum_d,), (sum_c, sum_a), (sum_d,), (sum_c,))):
        carry = lax.fori_loop(part * 16, part * 16 + 16, first_back, carry)
        for step in steps:
            next(step)
    shift, gain = carry
    shift1, gain1 = whole_sum(shift), whole_sum(gain) * rstd1
    sent_four = stats_send(3, shift1, gain1)
    total1 = stats_get(3, sent_four)
    next(sum_d)
    means = group_means(total1 * g1)
    steps_p = param_steps(
        jnp.concatenate([total1[1:2], total1[0:1], total2[1:2], total2[0:1], jnp.zeros((4, CP), F32)], axis=0)
    )
    next(steps_p)
    n_one, n_two = means[0:1] * rstd1, means[1:2] * (rstd1 * rstd1)

    def finish(n):
        r, q = n // 4, lax.rem(n, 4)
        p = pl.multiple_of(q * CHUNK, CHUNK)
        here = pl.ds(pl.multiple_of(n * CHUNK, CHUNK), CHUNK)
        v = gact[here, :] * scale1 - n_one - centred_one(r, p) * n_two
        gh[r, pl.ds(p, CHUNK), :] = (ub[r, pl.ds(p, CHUNK), :].astype(F32) + v[:, :C]).astype(BF16)

    pl.loop(0, 32)(finish)
    next(sum_c)
    next(sum_a)
    pl.loop(32, 64)(finish)
    outs = [pltpu.make_async_copy(gh, out_hbm.at[0], out_sem.at[3])]
    outs[0].start()
    next(sum_d)
    outs.append(next(sum_a))
    next(steps_p)
    next(sum_c)
    next(steps_p)
    next(sum_d)
    outs.append(next(sum_c))
    outs.append(next(sum_d))
    for copy in outs:
        copy.wait()


def unpack(g_hbm, o_hbm, g1_hbm, g2_hbm, t_hbm, g, out, o, ot, in_sem, out_sem, o_sem):
    first = pltpu.make_async_copy(o_hbm.at[0], o, o_sem.at[0])
    first.start()
    order = [(t, a) for t in range(2) for a in range(3)]
    reads = [pltpu.make_async_copy(g_hbm.at[t, a], g.at[t, a], in_sem.at[t, a]) for t, a in order]
    for copy in reads:
        copy.start()
    first.wait()

    @pl.loop(0, R)
    def _(r):
        ot[r] = widened(o[r].astype(F32)).T[:C].astype(BF16)

    writes = [pltpu.make_async_copy(ot, t_hbm.at[0], o_sem.at[1])]
    writes[0].start()
    for (t, a), read in zip(order, reads):
        read.wait()
        for c in range(3):
            b = 2 - c
            out[t, a, c, :, 0:256] = g[t, a, :, b * 256 : b * 256 + 256]
            x = g[t, a, :, 896:1024] if b == 2 else g[t, a, :, 768:896]
            if b == 1:
                x = pltpu.roll(x, 64, 1)
            out[t, a, c, :, 256:320] = x[:, 0:64]
        writes.append(pltpu.make_async_copy(out.at[t, a], (g2_hbm, g1_hbm)[t].at[a], out_sem.at[t, a]))
        writes[-1].start()
    for copy in writes:
        copy.wait()


def per_device(features, first_kernel, second_kernel, first_gain, first_shift, second_gain, second_shift, upstream):
    params = [first_gain, first_shift, second_gain, second_shift]
    hbm = pl.BlockSpec(memory_space=pl.ANY)
    vmem = pl.BlockSpec(memory_space=pltpu.VMEM)
    tile, packed, pg = pl.pallas_call(
        kernel,
        out_shape=(
            jax.ShapeDtypeStruct((1, R, W, C), BF16),
            jax.ShapeDtypeStruct((2, 3, C, PK), F32),
            jax.ShapeDtypeStruct((8, CP), F32),
        ),
        in_specs=[hbm, hbm, hbm, hbm, vmem, vmem, vmem, vmem],
        out_specs=(hbm, hbm, vmem),
        scratch_shapes=[
            pltpu.VMEM((R, W, C), BF16),
            pltpu.VMEM((R, W, C), BF16),
            pltpu.VMEM((R, W, C), BF16),
            pltpu.VMEM((3, 3, C, C), BF16),
            pltpu.VMEM((3, 3, C, C), BF16),
            pltpu.VMEM((PK, PK), BF16),
            pltpu.VMEM((PK, PK), BF16),
            pltpu.VMEM((R + 2, W + 16, CP), F32),
            pltpu.VMEM(((R + 2) * W, PK), BF16),
            pltpu.VMEM(((R + 2) * W, PK), BF16),
            pltpu.VMEM(((R + 2) * W, PK), F32),
            pltpu.VMEM((PX, CP), F32),
            pltpu.VMEM((PX, CP), BF16),
            pltpu.VMEM((C, PX), BF16),
            pltpu.VMEM((C, PX), BF16),
            pltpu.VMEM((2, 3, C, PK), F32),
            pltpu.VMEM((3, 160, PK), F32),
            pltpu.VMEM((3, 3, 40, PK), F32),
            pltpu.VMEM((3, 3, 40, 256), F32),
            pltpu.VMEM((3, 4, 40, 256), F32),
            pltpu.VMEM((2, 3, 160, 512), F32),
            pltpu.VMEM((2, 3, 3, 40, 512), F32),
            pltpu.VMEM((2, 3, 3, 40, 128), F32),
            pltpu.VMEM((2, 3, 4, 40, 128), F32),
            pltpu.VMEM((R, CP), F32),
            pltpu.VMEM((3, R, CP), BF16),
            pltpu.VMEM((3, 2, W, C), BF16),
            pltpu.VMEM((3, 3, R, CP), BF16),
            pltpu.VMEM((4, 8, 8, CP), F32),
            pltpu.VMEM((2, 4, 8, CP), F32),
            pltpu.SemaphoreType.DMA((3, R)),
            pltpu.SemaphoreType.DMA((4,)),
            pltpu.SemaphoreType.DMA((3, 5)),
            pltpu.SemaphoreType.DMA((3, 5)),
            pltpu.SemaphoreType.DMA((4, 7)),
            pltpu.SemaphoreType.DMA((4, 7)),
            pltpu.SemaphoreType.DMA((2, 3)),
            pltpu.SemaphoreType.DMA((2, 3)),
            pltpu.SemaphoreType.DMA((3, 7, 3, 3)),
            pltpu.SemaphoreType.DMA((3, 7, 3, 3)),
            pltpu.SemaphoreType.REGULAR((3, 3, 3)),
        ],
        compiler_params=pltpu.CompilerParams(
            collective_id=0, has_side_effects=True, vmem_limit_bytes=67_000_000
        ),
        name="resblock_backward",
    )(jnp.swapaxes(features, 2, 3), first_kernel, second_kernel, jnp.swapaxes(upstream, 2, 3), *params)
    grad = jax.ShapeDtypeStruct((3, 3, C, C), F32)
    g1, g2, input_grad = pl.pallas_call(
        unpack,
        out_shape=(grad, grad, jax.ShapeDtypeStruct((1, R, C, W), BF16)),
        in_specs=[hbm, hbm],
        out_specs=(hbm, hbm, hbm),
        scratch_shapes=[
            pltpu.VMEM((2, 3, C, PK), F32),
            pltpu.VMEM((2, 3, 3, C, C), F32),
            pltpu.VMEM((R, W, C), BF16),
            pltpu.VMEM((R, C, W), BF16),
            pltpu.SemaphoreType.DMA((2, 3)),
            pltpu.SemaphoreType.DMA((2, 3)),
            pltpu.SemaphoreType.DMA((2,)),
        ],
        name="unpack",
    )(packed, tile)
    return jnp.swapaxes(input_grad, 2, 3), g1, g2, pg[:4, :C]


def solution(mesh):
    tiles = P("batch", "row", "col", None)
    return jax.shard_map(
        per_device,
        mesh=mesh,
        in_specs=(tiles, P(), P(), P(), P(), P(), P(), tiles),
        out_specs=(tiles, P(), P(), P()),
        check_vma=False,
    )
```

```python
import jax
import jax.numpy as jnp
from jax import lax
from jax.experimental import pallas as pl
from jax.experimental.pallas import tpu as pltpu
from jax.sharding import PartitionSpec as P

GROUPS = 32
EPS = 1e-05
R, W, C, CP = 16, 128, 320, 384
PX = R * W
PK = 1024
CHUNK = 32
COUNT = float(64 * 256 * (C // GROUPS))
F32, BF16 = jnp.float32, jnp.bfloat16
MESH = pl.DeviceIdType.MESH


def widened(v):
    return jnp.concatenate([v, jnp.zeros((v.shape[0], CP - C), v.dtype)], axis=1)


def pack3(x0, x1, x2):
    t0, t1, t2 = (x[:, 256:384] for x in (x0, x1, x2))
    low = lax.broadcasted_iota(jnp.int32, t0.shape, 1) < 64
    mid = jnp.where(low, t0, pltpu.roll(t1, 64, 1))
    end = jnp.where(low, t2, 0.0)
    return jnp.concatenate([x0[:, :256], x1[:, :256], x2[:, :256], mid, end], axis=1)


def pack_weights(k_ref, dst_ref, block):
    for i in range(3):
        for s in range(5):
            parts = []
            for j in range(3):
                a, c = block(i, j)
                parts.append(widened(k_ref[a, c, 64 * s : 64 * s + 64, :].astype(F32)))
            start = i * 256 + 64 * s if s < 4 else 768 + 64 * i
            dst_ref[start : start + 64, :] = pack3(*parts).astype(BF16)
    dst_ref[960:1024, :] = jnp.zeros((64, PK), BF16)


def fold(x):
    return jnp.sum(x.reshape(-1, 8, CP), axis=0)


def whole_sum(acc):
    return jnp.sum(acc, axis=0, keepdims=True)


def sigmoid(v):
    return 1.0 / (1.0 + jnp.exp(-v))


def sigmoid_by_tanh(v):
    return 0.5 + 0.5 * jnp.tanh(0.5 * v)


def kernel(
    f_hbm, k1_hbm, k2_hbm, u_hbm, g1_ref, s1_ref, g2_ref, s2_ref,
    out_hbm, g_hbm, pg_ref,
    fb, ub, gh, k1, k2, w1, b2, pad, x3, u3, y, gact, hid, a1t, a2t, gs,
    c0buf, s10buf, s20buf, s30buf, c1buf, s11buf, s21buf, s31buf, edge32, edge, rowbuf, colbuf, statbuf, pgbuf,
    in_sem, out_sem, hs_sem, hr_sem, ss_sem, sr_sem, ps_sem, pr_sem, rs_sem, rr_sem, free_sem,
):
    row, col, batch = lax.axis_index("row"), lax.axis_index("col"), lax.axis_index("batch")
    me = row * 2 + col
    core, near, deep = lax.rem(batch, 2), lax.rem(batch // 2, 2), batch // 4
    spot = (row, col * 2 + near, deep)
    inner = near * 2 + core

    def device(x=row, hi=col, lo=near, z=deep, side=core):
        return {"batch": (z * 2 + lo) * 2 + side, "row": x, "col": hi}

    def along(axis, d):
        j = lax.rem(spot[axis] + d, 4)
        if axis == 0:
            return j, device(x=j)
        if axis == 1:
            return j, device(hi=j // 2, lo=lax.rem(j, 2))
        return j, device(z=j)

    def slot(r):
        return pl.ds(pl.multiple_of(lax.rem(r, 7) * C, 16), C), pl.ds(pl.multiple_of(r // 7 * 128, 128), 128)

    loads = [[], [], [], []]
    for n, (src, dst) in enumerate(((f_hbm, x3), (u_hbm, u3))):
        for r in range(R):
            rows, cols = slice(r % 7 * C, r % 7 * C + C), slice(r // 7 * 128, r // 7 * 128 + 128)
            loads[n].append(pltpu.make_async_copy(src.at[0, r], dst.at[rows, cols], in_sem.at[n, r]))
    for n, (src, dst) in enumerate(((k1_hbm, k1), (k2_hbm, k2))):
        loads[2 + n].append(pltpu.make_async_copy(src, dst, in_sem.at[2, n]))
    for group in loads:
        for copy in group:
            copy.start()

    def turned(ref, r):
        rows, cols = slot(r)
        v = ref[rows, cols].astype(F32)
        return jnp.concatenate([v, jnp.zeros((CP - C, W), F32)], axis=0).T

    def peer(d):
        other = lax.rem(me + d, 8)
        return device(x=other // 2, hi=lax.rem(other, 2))

    barrier = pltpu.get_barrier_semaphore()
    others = [peer(d) for d in range(1, 8)] + [along(2, d)[1] for d in range(1, 4)]
    others += [device(side=1 - core), device(lo=1 - near), device(lo=1 - near, hi=1 - col)]
    others += [device(lo=1 - near, side=1 - core)]
    for other in others:
        pl.semaphore_signal(barrier, inc=1, device_id=other, device_id_type=MESH)
    pl.semaphore_wait(barrier, len(others))

    def stats_send(phase, first, second):
        statbuf[phase, me] = jnp.concatenate([first, second, jnp.zeros((6, CP), F32)], axis=0)
        copies = []
        for d in range(1, 8):
            copy = pltpu.make_async_remote_copy(
                statbuf.at[phase, me], statbuf.at[phase, me],
                ss_sem.at[phase, d - 1], sr_sem.at[phase, d - 1],
                device_id=peer(d), device_id_type=MESH,
            )
            copy.start()
            copies.append(copy)
        return copies

    def stats_get(phase, copies):
        for copy in copies:
            copy.wait()
        total = statbuf[phase, 0]
        for n in range(1, 8):
            total = total + statbuf[phase, n]
        return total

    def send(sems, index, src, dst, target):
        copy = pltpu.make_async_remote_copy(
            src, dst, sems[0].at[index], sems[1].at[index], device_id=target, device_id_type=MESH
        )
        copy.start()
        return copy

    def wait_all(copies):
        for copy in copies:
            copy.wait()

    mine = pl.ds(pl.multiple_of(core * 160, 8), 160)
    theirs = pl.ds(pl.multiple_of((1 - core) * 160, 8), 160)

    def forty(j):
        return pl.ds(pl.multiple_of(core * 160 + j * 40, 8), 40)

    whole = (c0buf, s10buf, s20buf, s30buf)
    halves = [[ref.at[n] for ref in (c1buf, s11buf, s21buf, s31buf)] for n in range(2)]
    chains = ((0, 0, PK, whole), (1, 0, 512, halves[0]), (1, 512, 512, halves[1]))

    def pair_send(k, a):
        t, start, width, (cbuf, _, _, _) = chains[k]
        return send(
            (rs_sem, rr_sem), (k, 0, a, 0), gs.at[t, a, theirs, pl.ds(start, width)], cbuf.at[a],
            device(side=1 - core),
        )

    def reduce_steps(k, pair):
        t, start, width, (cbuf, s1buf, s2buf, s3buf) = chains[k]
        wide = pl.ds(start, width)

        def part(j):
            return pl.ds(pl.multiple_of(start + j * (width // 4), 128), width // 4)

        axes = [[(a + n) % 3 for n in range(3)] for a in range(3)]
        rows = [forty(spot[axes[a][0]]) for a in range(3)]
        cols = [part(spot[axes[a][1]]) for a in range(3)]
        flying = [[], [], []]

        def sent(stage, a, targets):
            for target in targets:
                pl.semaphore_signal(free_sem.at[k, stage, a], inc=1, device_id=target, device_id_type=MESH)

        def ring(a, n):
            return [along(axes[a][n], d) for d in range(1, 4)]

        def targets(a, n):
            return [target for _, target in ring(a, n)]

        def fly(stage, a, src, dst, target, d=0):
            flying[a].append(send((rs_sem, rr_sem), (k, stage, a, d), src, dst, target))

        def landed(a):
            wait_all(flying[a])
            flying[a].clear()

        for a in range(3):
            pair[a].wait()
            sent(0, a, [device(side=1 - core)])
            gs[t, a, mine, wide] += cbuf[a]
            for d, (j, target) in enumerate(ring(a, 0)):
                fly(1, a, gs.at[t, a, forty(j), wide], s1buf.at[a, d], target, d)
        yield
        for a in range(3):
            landed(a)
            sent(1, a, targets(a, 0))
            gs[t, a, rows[a], wide] += s1buf[a, 0] + s1buf[a, 1] + s1buf[a, 2]
            for d, (j, target) in enumerate(ring(a, 1)):
                fly(2, a, gs.at[t, a, rows[a], part(j)], s2buf.at[a, d], target, d)
        yield
        for a in range(3):
            landed(a)
            sent(2, a, targets(a, 1))
            slot = spot[axes[a][2]]
            s3buf[a, slot] = gs[t, a, rows[a], cols[a]] + (s2buf[a, 0] + s2buf[a, 1] + s2buf[a, 2])
            for d, target in enumerate(targets(a, 2)):
                fly(3, a, s3buf.at[a, slot], s3buf.at[a, slot], target, d)
        yield
        for a in range(3):
            landed(a)
            gs[t, a, rows[a], cols[a]] = (s3buf[a, 0] + s3buf[a, 1]) + (s3buf[a, 2] + s3buf[a, 3])
            pl.semaphore_wait(free_sem.at[k, 2, a], 3)
            block = gs.at[t, a, rows[a], cols[a]]
            for d, target in enumerate(targets(a, 1)):
                fly(4, a, block, block, target, d)
        yield
        for a in range(3):
            landed(a)
            pl.semaphore_wait(free_sem.at[k, 1, a], 3)
            block = gs.at[t, a, rows[a], wide]
            for d, target in enumerate(targets(a, 0)):
                fly(5, a, block, block, target, d)
        yield
        for a in range(3):
            landed(a)
            pl.semaphore_wait(free_sem.at[k, 0, a], 1)
            block = gs.at[t, a, mine, wide]
            fly(6, a, block, block, device(side=1 - core))
        yield
        for a in range(3):
            landed(a)
        copy = pltpu.make_async_copy(gs.at[t, :, :, wide], g_hbm.at[t, :, :, wide], out_sem.at[k])
        copy.start()
        yield copy

    def param_steps(value):
        slots = (deep, inner)
        for n in range(2):
            slot = slots[n]
            pgbuf[n, slot] = value
            flying = []
            for d in range(1, 4):
                j = lax.rem(slot + d, 4)
                target = device(z=j) if n == 0 else device(lo=j // 2, side=lax.rem(j, 2))
                flying.append(send((ps_sem, pr_sem), (n, d - 1), pgbuf.at[n, slot], pgbuf.at[n, slot], target))
            yield
            wait_all(flying)
            value = (pgbuf[n, 0] + pgbuf[n, 1]) + (pgbuf[n, 2] + pgbuf[n, 3])
        pg_ref[...] = value
        yield

    gi = lax.broadcasted_iota(jnp.int32, (CP, CP), 0)
    gj = lax.broadcasted_iota(jnp.int32, (CP, CP), 1)
    same = ((gi * 6554) >> 16 == (gj * 6554) >> 16) & (gi < C) & (gj < C)
    member = jnp.where(same, 1.0, 0.0).astype(BF16)

    def group_means(rows):
        high = rows.astype(BF16)
        rest = rows - high.astype(F32)
        middle = rest.astype(BF16)
        low = (rest - middle.astype(F32)).astype(BF16)
        parts = [jnp.dot(v, member, preferred_element_type=F32) for v in (high, middle, low)]
        return (parts[0] + (parts[1] + parts[2])) / COUNT

    def norm_stats(total):
        means = group_means(total)
        mean = means[0:1]
        rstd = lax.rsqrt(means[1:2] - mean * mean + EPS)
        return mean, rstd

    up, down = lax.rem(row + 3, 4), lax.rem(row + 1, 4)
    across = 1 - col

    def halo_send(phase, src):
        edge[phase] = edge32[...].astype(BF16)
        moves = (
            (src.at[0], rowbuf.at[phase, 1], up, col),
            (src.at[R - 1], rowbuf.at[phase, 0], down, col),
            (edge.at[phase], colbuf.at[phase, 0], down, across),
            (edge.at[phase], colbuf.at[phase, 1], row, across),
            (edge.at[phase], colbuf.at[phase, 2], up, across),
        )
        copies = []
        for n, (a, b, r, c) in enumerate(moves):
            copy = pltpu.make_async_remote_copy(
                a, b, hs_sem.at[phase, n], hr_sem.at[phase, n],
                device_id=device(x=r, hi=c), device_id_type=MESH,
            )
            copy.start()
            copies.append(copy)
        return copies

    def take_edge(r, x):
        edge32[pl.ds(r, 1), :] = jnp.where(col == 0, x[W - 1 : W], x[0:1])

    def halo_fill(phase, fn):
        above, below = row > 0, row < 3
        for n, slot, ok in ((0, 0, above), (1, R + 1, below)):
            v = fn(widened(rowbuf[phase, n].astype(F32)))
            pad[slot, 8 : 8 + W, :] = jnp.where(ok, v, 0.0)
        v0 = jnp.where(above, fn(colbuf[phase, 0].astype(F32)), 0.0)
        v1 = fn(colbuf[phase, 1].astype(F32))
        v2 = jnp.where(below, fn(colbuf[phase, 2].astype(F32)), 0.0)
        for slot in range(R + 2):
            line = v0[R - 1 : R] if slot == 0 else v2[0:1] if slot == R + 1 else v1[slot - 1 : slot]
            pad[slot, 7:8, :] = jnp.where(col == 1, line, 0.0)
            pad[slot, 8 + W : 9 + W, :] = jnp.where(col == 0, line, 0.0)

    def build(dst):
        @pl.loop(0, R + 2)
        def _(s):
            x = pad[s, 8 : 8 + W, :]
            place = lax.broadcasted_iota(jnp.int32, x.shape, 0)
            before = jnp.where(place == 0, pad[s, 7:8, :], pltpu.roll(x, 1, 0))
            after = jnp.where(place == W - 1, pad[s, 8 + W : 9 + W, :], pltpu.roll(x, W - 1, 0))
            dst[pl.ds(pl.multiple_of(s * W, W), W), :] = pack3(before, x, after).astype(BF16)

    def conv(src, weights, transposed, first=0, last=3):
        dims = (((1,), (1 if transposed else 0,)), ((), ()))

        @pl.loop(first, last)
        def _(s):
            rows = pl.ds(pl.multiple_of(s * 768, 768), 768)
            y[rows, :] = lax.dot_general(src[rows, :], weights[...], dims, preferred_element_type=F32)

    def combined(p, size):
        r0 = pl.ds(p, size)
        r1 = pl.ds(p + W, size)
        r2 = pl.ds(p + 2 * W, size)
        main = y[r0, 0:256] + y[r1, 256:512] + y[r2, 512:768]
        tail = y[r0, 768:896] + pltpu.roll(y[r1, 768:896], 64, 1) + y[r2, 896:1024]
        low = lax.broadcasted_iota(jnp.int32, tail.shape, 1) < 64
        return jnp.concatenate([main, jnp.where(low, tail, 0.0)], axis=1)

    def chunks(body, init):
        def step(n, carry):
            return body(pl.multiple_of(n * CHUNK, CHUNK), carry)

        return lax.fori_loop(0, PX // CHUNK, step, init)

    def kernel_dot(left, right, t, start, a):
        rows, cols = slice((2 - a) * W, (2 - a) * W + PX), slice(start, start + 512)
        gs[t, a, :, cols] = jnp.dot(left[...], right[rows, cols], preferred_element_type=F32)

    def kernel_grad(left, right, k):
        pair = []
        for a in range(3):
            kernel_dot(left, right, chains[k][0], chains[k][1], a)
            pair.append(pair_send(k, a))
        return reduce_steps(k, pair)

    zero = jnp.zeros((8, CP), F32)
    g1, s1, g2, s2 = (widened(v[...].reshape(1, C)) for v in (g1_ref, s1_ref, g2_ref, s2_ref))

    wait_all(loads[0])

    def first_stats(r, carry):
        total, square = carry
        x = turned(x3, r)
        fb[r] = x[:, :C].astype(BF16)
        take_edge(r, x)
        return total + fold(x), square + fold(x * x)

    total, square = lax.fori_loop(0, R, first_stats, (zero, zero))
    sent_one = stats_send(0, whole_sum(total), whole_sum(square))
    halo_one = halo_send(0, fb)

    wait_all(loads[1])

    @pl.loop(0, R)
    def _(r):
        x = turned(u3, r)
        ub[r] = x[:, :C].astype(BF16)
        take_edge(r, x)

    halo_up = halo_send(1, ub)
    wait_all(loads[2])
    pack_weights(k1, w1, lambda i, j: (j, i))
    wait_all(loads[3])
    pack_weights(k2, b2, lambda i, j: (2 - i, 2 - j))

    mean1, rstd1 = norm_stats(stats_get(0, sent_one))
    scale1 = rstd1 * g1
    for copy in halo_one:
        copy.wait()

    def act_one(x):
        v = (x - mean1) * scale1 + s1
        return (v * sigmoid_by_tanh(v)).astype(BF16).astype(F32)

    @pl.loop(0, R * 4)
    def _(n):
        r, q = n // 4, lax.rem(n, 4)
        p = pl.multiple_of(q * CHUNK, CHUNK)
        pad[r + 1, pl.ds(8 + p, CHUNK), :] = act_one(widened(fb[r, pl.ds(p, CHUNK), :].astype(F32)))

    halo_fill(0, act_one)
    build(x3)
    conv(x3, w1, False)

    def hidden_stats(p, carry):
        total, square = carry
        h = combined(p, CHUNK).astype(BF16)
        hid[pl.ds(p, CHUNK), :] = h
        h = h.astype(F32)
        return total + fold(h), square + fold(h * h)

    total, square = chunks(hidden_stats, (zero, zero))
    sent_two = stats_send(1, whole_sum(total), whole_sum(square))

    @pl.loop(0, R)
    def _(r):
        where = pl.ds(pl.multiple_of(r * W, W), W)
        a1t[:, where] = pad[r + 1, 8 : 8 + W, :].T[:C].astype(BF16)
        pad[r + 1, 8 : 8 + W, :] = widened(ub[r].astype(F32))

    wait_all(halo_up)
    halo_fill(1, lambda v: v)
    build(u3)
    conv(u3, b2, True)

    mean2, rstd2 = norm_stats(stats_get(1, sent_two))
    scale2 = rstd2 * g2

    def second_back(p, carry):
        shift, gain = carry
        here = pl.ds(p, CHUNK)
        q = pl.multiple_of(8 + lax.rem(p, W), 8)
        centred = hid[here, :].astype(F32) - mean2
        pre = centred * scale2 + s2
        s = sigmoid(pre)
        pad[p // W + 1, pl.ds(q, CHUNK), :] = pre * s
        gp = combined(p, CHUNK) * s * (1.0 + pre * (1.0 - s))
        gact[here, :] = gp
        return shift + fold(gp), gain + fold(gp * centred)

    shift, gain = chunks(second_back, (zero, zero))
    shift2, gain2 = whole_sum(shift), whole_sum(gain) * rstd2
    sent_three = stats_send(2, shift2, gain2)

    @pl.loop(0, R)
    def _(r):
        where = pl.ds(pl.multiple_of(r * W, W), W)
        a2t[:, where] = pad[r + 1, 8 : 8 + W, :].T[:C].astype(BF16)

    for a in range(3):
        kernel_dot(a2t, u3, 0, 0, a)
    total2 = stats_get(2, sent_three)
    means = group_means(total2 * g2)
    m1, m2 = means[0:1] * rstd2, means[1:2] * (rstd2 * rstd2)

    @pl.loop(0, R)
    def _(r):
        for q in range(W // CHUNK):
            here = pl.ds(pl.multiple_of(r * W + q * CHUNK, CHUNK), CHUNK)
            centred = hid[here, :].astype(F32) - mean2
            v = (gact[here, :] * scale2 - m1 - centred * m2).astype(BF16)
            gh[r, q * CHUNK : q * CHUNK + CHUNK, :] = v[:, :C]
            pad[r + 1, 8 + q * CHUNK : 8 + q * CHUNK + CHUNK, :] = v.astype(F32)
        edge32[pl.ds(r, 1), :] = jnp.where(
            col == 0, pad[r + 1, 7 + W : 8 + W, :], pad[r + 1, 8:9, :]
        )

    halo_gh = halo_send(2, gh)
    pair = []
    for a in range(3):
        kernel_dot(a2t, u3, 0, 512, a)
        pair.append(pair_send(0, a))
    sum_a = reduce_steps(0, pair)
    pack_weights(k1, w1, lambda i, j: (2 - i, 2 - j))
    wait_all(halo_gh)
    next(sum_a)
    halo_fill(2, lambda v: v)
    build(x3)
    sum_c = kernel_grad(a1t, x3, 1)
    sum_d = kernel_grad(a1t, x3, 2)
    next(sum_c)
    next(sum_a)
    conv(x3, w1, True, 0, 1)
    next(sum_d)
    next(sum_a)
    conv(x3, w1, True, 1, 3)
    next(sum_c)
    next(sum_a)

    def centred_one(r, p):
        return widened(fb[r, pl.ds(p, CHUNK), :].astype(F32)) - mean1

    def first_back(n, carry):
        shift, gain = carry
        r, q = n // 4, lax.rem(n, 4)
        p = pl.multiple_of(n * CHUNK, CHUNK)
        centred = centred_one(r, pl.multiple_of(q * CHUNK, CHUNK))
        pre = centred * scale1 + s1
        s = sigmoid_by_tanh(pre)
        gp = combined(p, CHUNK) * s * (1.0 + pre * (1.0 - s))
        gact[pl.ds(p, CHUNK), :] = gp
        return shift + fold(gp), gain + fold(gp * centred)

    carry = (zero, zero)
    for part, steps in enumerate(((sum_d,), (sum_c, sum_a), (sum_d,), (sum_c,))):
        carry = lax.fori_loop(part * 16, part * 16 + 16, first_back, carry)
        for step in steps:
            next(step)
    shift, gain = carry
    shift1, gain1 = whole_sum(shift), whole_sum(gain) * rstd1
    sent_four = stats_send(3, shift1, gain1)
    total1 = stats_get(3, sent_four)
    next(sum_d)
    means = group_means(total1 * g1)
    steps_p = param_steps(
        jnp.concatenate([total1[1:2], total1[0:1], total2[1:2], total2[0:1], jnp.zeros((4, CP), F32)], axis=0)
    )
    next(steps_p)
    n_one, n_two = means[0:1] * rstd1, means[1:2] * (rstd1 * rstd1)

    def finish(n):
        r, q = n // 4, lax.rem(n, 4)
        p = pl.multiple_of(q * CHUNK, CHUNK)
        here = pl.ds(pl.multiple_of(n * CHUNK, CHUNK), CHUNK)
        v = gact[here, :] * scale1 - n_one - centred_one(r, p) * n_two
        gh[r, pl.ds(p, CHUNK), :] = (ub[r, pl.ds(p, CHUNK), :].astype(F32) + v[:, :C]).astype(BF16)

    pl.loop(0, 32)(finish)
    next(sum_c)
    next(sum_a)
    pl.loop(32, 64)(finish)
    outs = [pltpu.make_async_copy(gh, out_hbm.at[0], out_sem.at[3])]
    outs[0].start()
    next(sum_d)
    outs.append(next(sum_a))
    next(steps_p)
    next(sum_c)
    next(steps_p)
    next(sum_d)
    outs.append(next(sum_c))
    outs.append(next(sum_d))
    for copy in outs:
        copy.wait()


def unpack(g_hbm, o_hbm, g1_hbm, g2_hbm, t_hbm, g, out, o, ot, in_sem, out_sem, o_sem):
    first = pltpu.make_async_copy(o_hbm.at[0], o, o_sem.at[0])
    first.start()
    order = [(t, a) for t in range(2) for a in range(3)]
    reads = [pltpu.make_async_copy(g_hbm.at[t, a], g.at[t, a], in_sem.at[t, a]) for t, a in order]
    for copy in reads:
        copy.start()
    writes = []
    for (t, a), read in zip(order, reads):
        read.wait()
        for c in range(3):
            b = 2 - c
            out[t, a, c, :, 0:256] = g[t, a, :, b * 256 : b * 256 + 256]
            x = g[t, a, :, 896:1024] if b == 2 else g[t, a, :, 768:896]
            if b == 1:
                x = pltpu.roll(x, 64, 1)
            out[t, a, c, :, 256:320] = x[:, 0:64]
        writes.append(pltpu.make_async_copy(out.at[t, a], (g2_hbm, g1_hbm)[t].at[a], out_sem.at[t, a]))
        writes[-1].start()
        if (t, a) == (0, 1):
            first.wait()

            @pl.loop(0, R)
            def _(r):
                ot[r] = widened(o[r].astype(F32)).T[:C].astype(BF16)

            writes.append(pltpu.make_async_copy(ot, t_hbm.at[0], o_sem.at[1]))
            writes[-1].start()
    for copy in writes:
        copy.wait()


def per_device(features, first_kernel, second_kernel, first_gain, first_shift, second_gain, second_shift, upstream):
    params = [first_gain, first_shift, second_gain, second_shift]
    hbm = pl.BlockSpec(memory_space=pl.ANY)
    vmem = pl.BlockSpec(memory_space=pltpu.VMEM)
    tile, packed, pg = pl.pallas_call(
        kernel,
        out_shape=(
            jax.ShapeDtypeStruct((1, R, W, C), BF16),
            jax.ShapeDtypeStruct((2, 3, C, PK), F32),
            jax.ShapeDtypeStruct((8, CP), F32),
        ),
        in_specs=[hbm, hbm, hbm, hbm, vmem, vmem, vmem, vmem],
        out_specs=(hbm, hbm, vmem),
        scratch_shapes=[
            pltpu.VMEM((R, W, C), BF16),
            pltpu.VMEM((R, W, C), BF16),
            pltpu.VMEM((R, W, C), BF16),
            pltpu.VMEM((3, 3, C, C), BF16),
            pltpu.VMEM((3, 3, C, C), BF16),
            pltpu.VMEM((PK, PK), BF16),
            pltpu.VMEM((PK, PK), BF16),
            pltpu.VMEM((R + 2, W + 16, CP), F32),
            pltpu.VMEM(((R + 2) * W, PK), BF16),
            pltpu.VMEM(((R + 2) * W, PK), BF16),
            pltpu.VMEM(((R + 2) * W, PK), F32),
            pltpu.VMEM((PX, CP), F32),
            pltpu.VMEM((PX, CP), BF16),
            pltpu.VMEM((C, PX), BF16),
            pltpu.VMEM((C, PX), BF16),
            pltpu.VMEM((2, 3, C, PK), F32),
            pltpu.VMEM((3, 160, PK), F32),
            pltpu.VMEM((3, 3, 40, PK), F32),
            pltpu.VMEM((3, 3, 40, 256), F32),
            pltpu.VMEM((3, 4, 40, 256), F32),
            pltpu.VMEM((2, 3, 160, 512), F32),
            pltpu.VMEM((2, 3, 3, 40, 512), F32),
            pltpu.VMEM((2, 3, 3, 40, 128), F32),
            pltpu.VMEM((2, 3, 4, 40, 128), F32),
            pltpu.VMEM((R, CP), F32),
            pltpu.VMEM((3, R, CP), BF16),
            pltpu.VMEM((3, 2, W, C), BF16),
            pltpu.VMEM((3, 3, R, CP), BF16),
            pltpu.VMEM((4, 8, 8, CP), F32),
            pltpu.VMEM((2, 4, 8, CP), F32),
            pltpu.SemaphoreType.DMA((3, R)),
            pltpu.SemaphoreType.DMA((4,)),
            pltpu.SemaphoreType.DMA((3, 5)),
            pltpu.SemaphoreType.DMA((3, 5)),
            pltpu.SemaphoreType.DMA((4, 7)),
            pltpu.SemaphoreType.DMA((4, 7)),
            pltpu.SemaphoreType.DMA((2, 3)),
            pltpu.SemaphoreType.DMA((2, 3)),
            pltpu.SemaphoreType.DMA((3, 7, 3, 3)),
            pltpu.SemaphoreType.DMA((3, 7, 3, 3)),
            pltpu.SemaphoreType.REGULAR((3, 3, 3)),
        ],
        compiler_params=pltpu.CompilerParams(
            collective_id=0, has_side_effects=True, vmem_limit_bytes=67_000_000
        ),
        name="resblock_backward",
    )(jnp.swapaxes(features, 2, 3), first_kernel, second_kernel, jnp.swapaxes(upstream, 2, 3), *params)
    grad = jax.ShapeDtypeStruct((3, 3, C, C), F32)
    g1, g2, input_grad = pl.pallas_call(
        unpack,
        out_shape=(grad, grad, jax.ShapeDtypeStruct((1, R, C, W), BF16)),
        in_specs=[hbm, hbm],
        out_specs=(hbm, hbm, hbm),
        scratch_shapes=[
            pltpu.VMEM((2, 3, C, PK), F32),
            pltpu.VMEM((2, 3, 3, C, C), F32),
            pltpu.VMEM((R, W, C), BF16),
            pltpu.VMEM((R, C, W), BF16),
            pltpu.SemaphoreType.DMA((2, 3)),
            pltpu.SemaphoreType.DMA((2, 3)),
            pltpu.SemaphoreType.DMA((2,)),
        ],
        name="unpack",
    )(packed, tile)
    return jnp.swapaxes(input_grad, 2, 3), g1, g2, pg[:4, :C]


def solution(mesh):
    tiles = P("batch", "row", "col", None)
    return jax.shard_map(
        per_device,
        mesh=mesh,
        in_specs=(tiles, P(), P(), P(), P(), P(), P(), tiles),
        out_specs=(tiles, P(), P(), P()),
        check_vma=False,
    )
```
